128 devices in a mesh: prow: 8 (over z, core), pcol: 16 (over x, y).
Axes of the slice: x: 4, y: 4, z: 4, core: 2. Of those that a mesh axis runs over, the one named last changes fastest.
Arguments:
- panel_pos: float32 [3, 256], replicated
- trail_pos: float32 [3, 8192], P(None, ('prow', 'pcol')), as said below
- slot_block: int32 [32], replicated, may hold values from 0 to 31, each once
Outputs:
- panel_diag: float32 [768, 768], replicated
- panel_below: float32 [24576, 768], P(('prow', 'pcol'))
- trailing: float32 [24576, 24576], P('prow', 'pcol')
The draws below stay inside these ranges and needn't reach their ends.
Inputs may be any that keep to these rules, and one draw needn't show every extreme that they name: `slot_block`: every trailing panel is named by exactly one slot. Any two particles of panel_pos and trail_pos together are 0.5 or more apart.
All inputs are finite; a program needn't handle non-finite values.
Results may differ from the reference program's by a relative error of at most 0.0003.
Values sent between devices are 32-bit elements; how exact they have to be, the bound alone decides.
A program may use at most 192 MiB of HBM per device.

```python
import jax
import jax.numpy as jnp
from jax import lax

PB = 256
K = 32


def particle_lattice(key):
    particles = (K + 1) * PB
    lattice_side = 1
    while lattice_side ** 3 < particles:
        lattice_side = lattice_side + 1
    base_key = jax.random.fold_in(key, 7)
    chosen_sites = jax.random.permutation(jax.random.fold_in(base_key, 1), lattice_side ** 3)[:particles]
    lattice_sites = jnp.stack([chosen_sites // (lattice_side * lattice_side), chosen_sites // lattice_side % lattice_side, chosen_sites % lattice_side]).astype(jnp.float32)
    noise_key = jax.random.fold_in(base_key, 2)
    jitter = jax.random.uniform(noise_key, (3, particles), jnp.float32, -0.25, 0.25)
    return lattice_sites + jitter


def draw_panel_pos(key, part):
    return particle_lattice(key)[:, :PB]


def draw_trail_pos(key, part):
    return particle_lattice(key)[:, PB:]


def setup_inputs(seed: int = 0) -> dict:
    key_list = jax.random.split(jax.random.key(seed), 4)
    panel_pos = draw_panel_pos(jax.random.fold_in(key_list[3], 71), 0)
    trail_pos = draw_trail_pos(jax.random.fold_in(key_list[3], 71), 0)
    slot_block = jax.random.permutation(key_list[2], K).astype(jnp.int32)
    return dict(panel_pos=panel_pos, trail_pos=trail_pos, slot_block=slot_block)


radius = 0.25

def pair_terms(difference, same_particle):
    squared = lax.optimization_barrier(jnp.sum(difference * difference, axis=0))
    safe_square = jnp.where(same_particle, 1.0, squared)
    inverse_r = lax.rsqrt(safe_square)
    radius_ratio = radius * radius * inverse_r * inverse_r
    isotropic = jnp.where(same_particle, 1.0, 0.75 * radius * inverse_r * (1.0 + radius_ratio * 2.0 / 3.0))
    directed = jnp.where(same_particle, 0.0, 0.75 * radius * inverse_r * inverse_r * inverse_r * (1.0 - 2.0 * radius_ratio))
    return (isotropic, directed)

def block_tiles(row_pos, row_ids, col_pos, col_ids):
    difference = row_pos[:, :, :, None, None] - col_pos[:, None, None, :, :]
    same_particle = row_ids[:, :, None, None] == col_ids[None, None, :, :]
    isotropic, directed = pair_terms(difference, same_particle)
    identity = jnp.eye(3, dtype=difference.dtype)
    tensor = identity[:, :, None, None, None, None] * isotropic[None, None] + directed[None, None] * difference[:, None] * difference[None, :]
    tensor = jnp.transpose(tensor, (2, 0, 3, 4, 1, 5))
    return tensor.reshape(row_pos.shape[1] * 3 * PB, col_pos.shape[1] * 3 * PB)

def row_tiles(row_pos, component, panel):
    difference = row_pos[:, :, None] - panel[:, None, :]
    same_particle = jnp.zeros(difference.shape[1:], dtype=jnp.bool_)
    isotropic, directed = pair_terms(difference, same_particle)
    select = (component[None, :] == lax.iota(jnp.int32, 3)[:, None]).astype(difference.dtype)
    projected = lax.optimization_barrier(jnp.sum(select[:, :, None] * difference, axis=0))
    tensor = select[:, :, None] * isotropic[None] + directed[None] * projected[None] * difference
    return jnp.transpose(tensor, (1, 0, 2)).reshape(row_pos.shape[1], 3 * PB)

def row_layout(global_rows):
    width = 3 * PB
    block_index = global_rows // width
    within = global_rows % width
    component = (within // PB).astype(jnp.int32)
    particle = (block_index * PB + within % PB).astype(jnp.int32)
    return (component, particle)

def outer_rows(left_rows, right_rows):
    return lax.dot_general(left_rows.astype(jnp.float32), right_rows.astype(jnp.float32), (((1,), (1,)), ((), ())), precision=lax.Precision.HIGHEST, preferred_element_type=jnp.float32)

def reference(panel_pos, trail_pos, slot_block):
    width = 3 * PB
    panels = slot_block.shape[0]
    sorted_pos = trail_pos.reshape(3, panels, PB)[:, slot_block].reshape(3, panels * PB)
    panel_ids = lax.iota(jnp.int32, PB).reshape(1, PB)
    diag_block = block_tiles(panel_pos.reshape(3, 1, PB), panel_ids, panel_pos.reshape(3, 1, PB), panel_ids)
    factor = jnp.linalg.cholesky(diag_block)
    inverse = jax.scipy.linalg.solve_triangular(factor, jnp.eye(width, dtype=factor.dtype), lower=True)
    component, particle = row_layout(lax.iota(jnp.int32, panels * width))
    below_block = row_tiles(jnp.take(sorted_pos, particle, axis=1), component, panel_pos)
    panel_below = outer_rows(below_block, inverse)
    blocks = sorted_pos.reshape(3, panels, PB)
    slot_ids = lax.iota(jnp.int32, panels * PB).reshape(panels, PB)

    def one_block(block_index):
        row_pos = lax.dynamic_slice_in_dim(blocks, block_index, 1, 1)
        row_ids = lax.dynamic_slice_in_dim(slot_ids, block_index, 1, 0)
        pair_tiles = block_tiles(row_pos, row_ids, blocks, slot_ids)
        left_rows = lax.dynamic_slice_in_dim(panel_below, block_index * width, width, 0)
        return pair_tiles - outer_rows(left_rows, panel_below)
    trailing = lax.map(one_block, lax.iota(jnp.int32, panels)).reshape(panels * width, panels * width)
    return (factor, panel_below, trailing)
```

```python
import functools
import jax
import jax.numpy as jnp
from jax import lax
from jax.experimental import pallas as pl
from jax.experimental.pallas import tpu as pltpu
from jax.sharding import PartitionSpec as P

RADIUS = 0.25
F32, BF16 = jnp.float32, jnp.bfloat16
NT = (((1,), (1,)), ((), ()))
NN = (((1,), (0,)), ((), ()))
TN = (((0,), (0,)), ((), ()))


def split(x):
    hi = x.astype(BF16)
    return hi, (x - hi.astype(F32)).astype(BF16)


def dot3(a, b, dims):
    ah, al = split(a)
    bh, bl = split(b)
    d = functools.partial(lax.dot_general, dimension_numbers=dims, preferred_element_type=F32)
    return d(ah, bh) + (d(al, bh) + d(ah, bl))


def pair_terms(rows, cols):
    diff = [r - c for r, c in zip(rows, cols)]
    squared = diff[0] * diff[0] + diff[1] * diff[1] + diff[2] * diff[2]
    same = squared < 0.01
    inv = lax.rsqrt(jnp.where(same, 1.0, squared))
    inv2 = inv * inv
    t = (0.75 * RADIUS) * inv
    t2 = t * inv2
    iso = jnp.where(same, 1.0, t + (RADIUS * RADIUS * 2.0 / 3.0) * t2)
    directed = t2 * (1.0 - (2.0 * RADIUS * RADIUS) * inv2)
    return diff, iso, directed


def tensor_entries(rows, cols):
    diff, iso, directed = pair_terms(rows, cols)
    g = [directed * d for d in diff]
    e = {}
    for i in range(3):
        for j in range(i, 3):
            v = g[i] * diff[j]
            if i == j:
                v = v + iso
            e[i, j] = e[j, i] = v
    return e


def bsub(row):
    return jnp.broadcast_to(row, (8, row.shape[-1]))


def factor_block(d_ref):
    sub = lax.broadcasted_iota(jnp.int32, (8, 128), 0)
    n = 16
    ta = [d_ref[8 * s : 8 * s + 8, :128] for s in range(n)]
    ti = [d_ref[8 * s : 8 * s + 8, 128:] for s in range(n)]
    for t in range(n):
        cs = {s: [jnp.broadcast_to(ta[s][:, 8 * t + k : 8 * t + k + 1], (8, 128)) for k in range(8)] for s in range(t, n)}
        for j in range(8):
            rs = lax.rsqrt(bsub(cs[t][j][j : j + 1, :]))
            mt = cs[t][j] * rs
            mm = jnp.where(sub > j, mt, 0.0)
            sp = {k: bsub(mt[k : k + 1, :]) for k in range(j + 1, 8)}
            ua = bsub(ta[t][j : j + 1, :]) * rs
            ui = bsub(ti[t][j : j + 1, :]) * rs
            ta[t] = jnp.where(sub == j, ua, ta[t] - mm * ua)
            ti[t] = jnp.where(sub == j, ui, ti[t] - mm * ui)
            for k in range(j + 1, 8):
                cs[t][k] = cs[t][k] - mm * sp[k]
            for s in range(t + 1, n):
                m = cs[s][j] * rs
                ta[s] = ta[s] - m * ua
                ti[s] = ti[s] - m * ui
                for k in range(j + 1, 8):
                    cs[s][k] = cs[s][k] - m * sp[k]
        d_ref[8 * t : 8 * t + 8, :128] = ta[t]
        d_ref[8 * t : 8 * t + 8, 128:] = ti[t]


def cat_store(ref, rows, chunk, hi, lo, order):
    base = 768 * chunk
    for i, w in enumerate(order):
        ref[rows, base + 256 * i : base + 256 * i + 256] = hi if w == "h" else lo


def chol(panel_ref, panel_t, m_ref, d_ref, l_ref, xcat):
    m_ref[:, 768:] = jnp.zeros((768, 768), F32)
    for r in range(0, 256, 32):
        rows = [panel_t[r : r + 32, c : c + 1] for c in range(3)]
        cols = [panel_ref[c : c + 1, :] for c in range(3)]
        e = tensor_entries(rows, cols)
        for i in range(3):
            for j in range(3):
                m_ref[256 * i + r : 256 * i + r + 32, 256 * j : 256 * j + 256] = e[i, j]
    eye = (lax.broadcasted_iota(jnp.int32, (128, 128), 0) == lax.broadcasted_iota(jnp.int32, (128, 128), 1)).astype(F32)
    upper = lax.broadcasted_iota(jnp.int32, (128, 128), 0) <= lax.broadcasted_iota(jnp.int32, (128, 128), 1)
    l_ref[...] = jnp.zeros((768, 768), F32)
    xcat[...] = jnp.zeros(xcat.shape, BF16)

    def panel(p, _):
        base = pl.multiple_of(128 * p, 128)
        nxt = pl.multiple_of(128 * p + 128, 128)
        d_ref[:, :128] = m_ref[pl.ds(base, 128), pl.ds(base, 128)]
        d_ref[:, 128:] = eye
        factor_block(d_ref)
        x = d_ref[:, 128:]
        row = dot3(x, m_ref[pl.ds(base, 128), pl.ds(nxt, 640)], NN)
        m_ref[pl.ds(base, 128), pl.ds(base, 128)] = jnp.where(upper, d_ref[:, :128], 0.0)
        m_ref[pl.ds(base, 128), pl.ds(nxt, 640)] = row
        m_ref[pl.ds(base, 128), pl.ds(768 + base, 128)] = x

        def update(r, _):
            at = pl.multiple_of(128 * r, 128)
            lt = m_ref[pl.ds(base, 128), pl.ds(at, 128)]
            m_ref[pl.ds(at, 128), pl.ds(nxt, 768)] -= dot3(lt, m_ref[pl.ds(base, 128), pl.ds(nxt, 768)], TN)
            return 0

        lax.fori_loop(p + 1, 6, update, 0)
        return 0

    lax.fori_loop(0, 6, panel, 0)
    for p in range(6):
        for q in range(p, 6):
            l_ref[128 * q : 128 * q + 128, 128 * p : 128 * p + 128] = m_ref[128 * p : 128 * p + 128, 128 * q : 128 * q + 128].T
    for k in range(3):
        hi, lo = split(m_ref[256 * k :, 768 + 256 * k : 1024 + 256 * k])
        cat_store(xcat, slice(256 * k, 768), k, hi, lo, "hhl")


def panel_rows(rows, panel_ref, bcat, xcat, emit):
    for r in range(0, 128, 32):
        e = tensor_entries(rows(r, 32), [panel_ref[c : c + 1, :] for c in range(3)])
        for i in range(3):
            for j in range(3):
                hi, lo = split(e[i, j])
                cat_store(bcat, slice(128 * i + r, 128 * i + r + 32), j, hi, lo, "hlh")
    for n in range(3):
        k = 768 * (n + 1)
        v = lax.dot_general(bcat[:, :k], xcat[256 * n : 256 * n + 256, :k], NT, preferred_element_type=F32)
        emit(n, v)


def kernel(slot_ref, panel_ref, g_ref, l_ref, own_ref, out_ref, m_ref, d_ref, xcat, ccat, rcat, bcat, rowt, colt, colp, pt, ids):
    step = pl.program_id(0)
    lane = lax.broadcasted_iota(jnp.int32, (8, 128), 1)
    prow, pcol = ids()

    def lane_tile(k, half):
        d = 4 * k + 2 * half
        a = jnp.concatenate([g_ref[(d % 16), d // 16], jnp.zeros((5, 64), F32)], axis=0)
        d = d + 1
        b = jnp.concatenate([g_ref[(d % 16), d // 16], jnp.zeros((5, 64), F32)], axis=0)
        return jnp.concatenate([a, b], axis=1)

    def transposed(tile):
        return jnp.concatenate([tile, jnp.zeros((120, 128), F32)], axis=0).T

    @pl.when(step == 0)
    def _():
        for half in range(2):
            tile = panel_ref[:, 128 * half : 128 * half + 128]
            pt[128 * half : 128 * half + 128, :] = transposed(tile)

        def rows_of(i, _):
            k = slot_ref[prow * 4 + i // 2]
            rowt[pl.ds(pl.multiple_of(i * 128, 128), 128), :] = transposed(lane_tile(k, i % 2))
            return 0

        lax.fori_loop(0, 8, rows_of, 0)
        for i in range(4):
            k = slot_ref[pcol * 2 + i // 2]
            tile = lane_tile(k, i % 2)
            colp[:, 128 * i : 128 * i + 128] = tile
            colt[128 * i : 128 * i + 128, :] = transposed(tile)
        chol(panel_ref, pt, m_ref, d_ref, l_ref, xcat)

        def col_rows(i, _):
            at = pl.multiple_of(i * 128, 128)
            dst = (i // 2) * 768 + (i % 2) * 128

            def emit(n, v):
                hi, lo = split(v)
                for j in range(3):
                    cat_store(ccat, pl.ds(pl.multiple_of(dst + 256 * j, 128), 128), n,
                              hi[128 * j : 128 * j + 128], lo[128 * j : 128 * j + 128], "hhl")

            panel_rows(lambda r, m: [colt[pl.ds(at + r, m), c : c + 1] for c in range(3)], panel_ref, bcat, xcat, emit)
            return 0

        lax.fori_loop(0, 4, col_rows, 0)

    c = step % 2
    tile = step // 2
    at = pl.multiple_of(tile * 128, 128)

    @pl.when(c == 0)
    def _():
        def emit(n, v):
            hi, lo = split(v)
            cat_store(rcat, slice(None), n, hi, lo, "hlh")
            for i in range(3):
                for h in range(2):
                    piece = i * 4 + (tile % 2) * 2 + h

                    @pl.when((tile // 2 == pcol // 4) & (piece // 3 == pcol % 4))
                    def _():
                        own_ref[pl.ds(pl.multiple_of((piece % 3) * 64, 64), 64), 256 * n : 256 * n + 256] = v[128 * i + 64 * h : 128 * i + 64 * h + 64]

        panel_rows(lambda r, m: [rowt[pl.ds(at + r, m), k : k + 1] for k in range(3)], panel_ref, bcat, xcat, emit)

    crow = pl.multiple_of(c * 768, 256)
    for j in range(3):
        v = lax.dot_general(rcat[...], ccat[pl.ds(crow + 256 * j, 256), :], NT, preferred_element_type=F32)
        out_ref[0, :, :, 256 * j : 256 * j + 256] = v.reshape(3, 128, 256)
    cc = pl.multiple_of(c * 256, 256)
    for r in range(0, 128, 32):
        rows = [rowt[pl.ds(at + r, 32), k : k + 1] for k in range(3)]
        cols = [colp[k : k + 1, pl.ds(cc, 256)] for k in range(3)]
        e = tensor_entries(rows, cols)
        for i in range(3):
            for j in range(3):
                out_ref[0, i, r : r + 32, 256 * j : 256 * j + 256] = e[i, j] - out_ref[0, i, r : r + 32, 256 * j : 256 * j + 256]


def main_call(slot_block, panel_pos, gathered, ids):
    panel8 = jnp.pad(panel_pos, ((0, 5), (0, 0)))
    whole = lambda s: (0, 0)
    l, own, out = pl.pallas_call(
        functools.partial(kernel, ids=ids),
        grid=(16,),
        in_specs=[
            pl.BlockSpec(memory_space=pltpu.SMEM),
            pl.BlockSpec((8, 256), whole),
            pl.BlockSpec((16, 8, 3, 64), lambda s: (0, 0, 0, 0)),
        ],
        out_specs=[
            pl.BlockSpec((768, 768), whole),
            pl.BlockSpec((192, 768), whole),
            pl.BlockSpec((1, 3, 128, 768), lambda s: (s // 4, 0, (s // 2) % 2, s % 2)),
        ],
        out_shape=[
            jax.ShapeDtypeStruct((768, 768), F32),
            jax.ShapeDtypeStruct((192, 768), F32),
            jax.ShapeDtypeStruct((4, 3, 256, 1536), F32),
        ],
        scratch_shapes=[
            pltpu.VMEM((768, 1536), F32),
            pltpu.VMEM((128, 256), F32),
            pltpu.VMEM((768, 2304), BF16),
            pltpu.VMEM((1536, 2304), BF16),
            pltpu.VMEM((384, 2304), BF16),
            pltpu.VMEM((384, 2304), BF16),
            pltpu.VMEM((1024, 128), F32),
            pltpu.VMEM((512, 128), F32),
            pltpu.VMEM((8, 512), F32),
            pltpu.VMEM((256, 128), F32),
        ],
        compiler_params=pltpu.CompilerParams(dimension_semantics=("arbitrary",), vmem_limit_bytes=62 << 20),
        name="panel_step",
    )(slot_block, panel8, gathered)
    return l, own, out.reshape(3072, 1536)


MESH = pl.DeviceIdType.MESH


def gather_kernel(n_rows, n_cols, own_ref, out_ref, send_sem, recv_sem, local_sem):
    r = lax.axis_index("prow")
    c = lax.axis_index("pcol")
    local = pltpu.make_async_copy(own_ref, out_ref.at[c, r], local_sem)
    local.start()
    barrier = pltpu.get_barrier_semaphore()
    for i in range(1, n_rows):
        pl.semaphore_signal(barrier, inc=1, device_id=(lax.rem(r + i, n_rows), c), device_id_type=MESH)
    for i in range(1, n_cols):
        pl.semaphore_signal(barrier, inc=1, device_id=(r, lax.rem(c + i, n_cols)), device_id_type=MESH)
    pl.semaphore_wait(barrier, n_rows + n_cols - 2)
    first = [
        pltpu.make_async_remote_copy(
            src_ref=own_ref,
            dst_ref=out_ref.at[c, r],
            send_sem=send_sem.at[i],
            recv_sem=recv_sem.at[i],
            device_id=(lax.rem(r + i, n_rows), c),
            device_id_type=MESH,
        )
        for i in range(1, n_rows)
    ]
    for copy in first:
        copy.start()
    local.wait()
    for copy in first:
        copy.wait()
    second = [
        pltpu.make_async_remote_copy(
            src_ref=out_ref.at[c],
            dst_ref=out_ref.at[c],
            send_sem=send_sem.at[n_rows + i],
            recv_sem=recv_sem.at[n_rows + i],
            device_id=(r, lax.rem(c + i, n_cols)),
            device_id_type=MESH,
        )
        for i in range(1, n_cols)
    ]
    for copy in second:
        copy.start()
    for copy in second:
        copy.wait()


def gather_positions(own):
    n_rows, n_cols = lax.axis_size("prow"), lax.axis_size("pcol")
    return pl.pallas_call(
        functools.partial(gather_kernel, n_rows, n_cols),
        out_shape=jax.ShapeDtypeStruct((n_cols, n_rows) + own.shape, own.dtype),
        in_specs=[pl.BlockSpec(memory_space=pltpu.VMEM)],
        out_specs=pl.BlockSpec(memory_space=pltpu.VMEM),
        scratch_shapes=[
            pltpu.SemaphoreType.DMA((n_rows + n_cols,)),
            pltpu.SemaphoreType.DMA((n_rows + n_cols,)),
            pltpu.SemaphoreType.DMA,
        ],
        compiler_params=pltpu.CompilerParams(collective_id=0, has_side_effects=True),
        name="gather_positions",
    )(own)


def shards(panel_pos, trail_pos, slot_block):
    gathered = gather_positions(trail_pos)
    return main_call(slot_block, panel_pos, gathered, lambda: (lax.axis_index("prow"), lax.axis_index("pcol")))


def solution(mesh):
    return jax.shard_map(
        shards,
        mesh=mesh,
        in_specs=(P(), P(None, ("prow", "pcol")), P()),
        out_specs=(P(), P(("prow", "pcol"), None), P("prow", "pcol")),
        check_vma=False,
    )
```

```python
import functools
import jax
import jax.numpy as jnp
from jax import lax
from jax.experimental import pallas as pl
from jax.experimental.pallas import tpu as pltpu
from jax.sharding import PartitionSpec as P

RADIUS = 0.25
F32, BF16, F8 = jnp.float32, jnp.bfloat16, jnp.float8_e4m3fn
NT = (((1,), (1,)), ((), ()))
NN = (((1,), (0,)), ((), ()))
TN = (((0,), (0,)), ((), ()))


def split(x):
    hi = x.astype(BF16)
    return hi, (x - hi.astype(F32)).astype(BF16)


def dot3(a, b, dims):
    ah, al = split(a)
    bh, bl = split(b)
    d = functools.partial(lax.dot_general, dimension_numbers=dims, preferred_element_type=F32)
    return d(ah, bh) + (d(al, bh) + d(ah, bl))


def pair_terms(rows, cols):
    diff = [r - c for r, c in zip(rows, cols)]
    squared = diff[0] * diff[0] + diff[1] * diff[1] + diff[2] * diff[2]
    same = squared < 0.01
    inv = lax.rsqrt(jnp.where(same, 1.0, squared))
    inv2 = inv * inv
    t = (0.75 * RADIUS) * inv
    t2 = t * inv2
    iso = jnp.where(same, 1.0, t + (RADIUS * RADIUS * 2.0 / 3.0) * t2)
    directed = t2 * (1.0 - (2.0 * RADIUS * RADIUS) * inv2)
    return diff, iso, directed


def tensor_entries(rows, cols):
    diff, iso, directed = pair_terms(rows, cols)
    g = [directed * d for d in diff]
    e = {}
    for i in range(3):
        for j in range(i, 3):
            v = g[i] * diff[j]
            if i == j:
                v = v + iso
            e[i, j] = e[j, i] = v
    return e


def bsub(row):
    return jnp.broadcast_to(row, (8, row.shape[-1]))


def rep(tile, rows):
    return jnp.concatenate([tile] * (rows // 8), axis=0)


def first_tile(tile, rest):
    return tile if rest.shape[0] == 8 else jnp.concatenate([tile, rest[8:]], axis=0)


def factor_block(d_ref):
    sub = lax.broadcasted_iota(jnp.int32, (8, 128), 0)
    a = d_ref[:, :128]
    inv = d_ref[:, 128:]
    for t in range(16):
        n = 128 - 8 * t
        cs = [jnp.broadcast_to(a[:, 8 * t + k : 8 * t + k + 1], (n, 128)) for k in range(8)]
        for j in range(8):
            rs = lax.rsqrt(bsub(cs[j][j : j + 1, :]))
            m = cs[j] * rep(rs, n)
            sp = [rep(bsub(m[k : k + 1, :]), n) for k in range(j + 1, 8)]
            m = first_tile(jnp.where(sub > j, m[:8], 0.0), m)
            ua = bsub(a[j : j + 1, :]) * rs
            ui = bsub(inv[j : j + 1, :]) * rs
            a = a - m * rep(ua, n)
            a = first_tile(jnp.where(sub == j, ua, a[:8]), a)
            inv = inv - m * rep(ui, n)
            inv = first_tile(jnp.where(sub == j, ui, inv[:8]), inv)
            for k in range(j + 1, 8):
                cs[k] = cs[k] - m * sp[k - j - 1]
        d_ref[8 * t : 8 * t + 8, :128] = a[:8]
        d_ref[8 * t : 8 * t + 8, 128:] = inv[:8]
        if t < 15:
            a, inv = a[8:], inv[8:]


def cat_store(ref, rows, chunk, hi, lo, order):
    base = 768 * chunk
    for i, w in enumerate(order):
        ref[rows, base + 256 * i : base + 256 * i + 256] = hi if w == "h" else lo


def chol(panel_ref, panel_t, m_ref, d_ref, row_buf, lt_buf, l_buf, xcat, after):
    m_ref[:, 768:] = jnp.zeros((m_ref.shape[0], 768), F32)
    m_ref[768:, :768] = jnp.zeros((m_ref.shape[0] - 768, 768), F32)
    for r in range(0, 256, 32):
        rows = [panel_t[r : r + 32, c : c + 1] for c in range(3)]
        cols = [panel_ref[c : c + 1, :] for c in range(3)]
        e = tensor_entries(rows, cols)
        for i in range(3):
            for j in range(3):
                m_ref[256 * i + r : 256 * i + r + 32, 256 * j : 256 * j + 256] = e[i, j]
    rows_at = lax.broadcasted_iota(jnp.int32, (128, 128), 0)
    cols_at = lax.broadcasted_iota(jnp.int32, (128, 128), 1)
    eye = (rows_at == cols_at).astype(F32)
    l_buf[...] = jnp.zeros(l_buf.shape, F32)
    xcat[...] = jnp.zeros(xcat.shape, BF16)
    row_buf[...] = jnp.zeros(row_buf.shape, F32)
    lt_buf[...] = jnp.zeros(lt_buf.shape, F32)
    d_ref[:, :128] = m_ref[:128, :128]
    d_ref[:, 128:] = eye

    def panel(p, _):
        base = pl.multiple_of(128 * p, 128)
        nxt = pl.multiple_of(128 * p + 128, 128)
        for i in range(5):
            at = pl.multiple_of(base + 128 * i, 128)
            m_ref[pl.ds(at, 128), pl.ds(base, 768)] -= dot3(lt_buf[128 * i : 128 * i + 128, :], row_buf[...], NN)
        factor_block(d_ref)
        x = d_ref[:, 128:]
        l_buf[pl.ds(base, 128), pl.ds(base, 128)] = jnp.where(rows_at >= cols_at, d_ref[:, :128].T, 0.0)
        row = dot3(x, m_ref[pl.ds(base, 128), pl.ds(nxt, 640)], NN)
        row_buf[:, :640] = row
        row_buf[:, 640:] = x
        m_ref[pl.ds(base, 128), pl.ds(nxt, 640)] = row
        m_ref[pl.ds(base, 128), pl.ds(768 + base, 128)] = x
        first = row[:, :128].T
        d_ref[:, :128] = m_ref[pl.ds(nxt, 128), pl.ds(nxt, 128)] - dot3(first, row[:, :128], NN)
        d_ref[:, 128:] = eye
        lt_buf[:128, :] = first
        l_buf[pl.ds(nxt, 128), pl.ds(base, 128)] = first
        for i in range(1, 5):
            lt = row[:, 128 * i : 128 * i + 128].T
            lt_buf[128 * i : 128 * i + 128, :] = lt
            l_buf[pl.ds(pl.multiple_of(nxt + 128 * i, 128), 128), pl.ds(base, 128)] = lt
        after(p)
        return 0

    lax.fori_loop(0, 6, panel, 0)
    for k in range(3):
        hi, lo = split(m_ref[256 * k : 768, 768 + 256 * k : 1024 + 256 * k])
        cat_store(xcat, slice(256 * k, 768), k, hi, lo, "hhl")


def panel_entries(rows, panel_ref, bcat):
    for r in range(0, 128, 32):
        e = tensor_entries(rows(r, 32), [panel_ref[c : c + 1, :] for c in range(3)])
        for i in range(3):
            for j in range(3):
                hi, lo = split(e[i, j])
                cat_store(bcat, slice(128 * i + r, 128 * i + r + 32), j, hi, lo, "hlh")


def panel_dot(bcat, xcat, n):
    k = 768 * (n + 1)
    return lax.dot_general(bcat[:, :k], xcat[256 * n : 256 * n + 256, :k], NT, preferred_element_type=F32)


S_HI = 256.0
S_LO = 131072.0


def split_store(v, n, row_sets, hi_ref, f8_ref, lo_ref, flip):
    hi = v.astype(BF16)
    back = hi.astype(F32)
    lo = v - back
    h8 = (back * S_HI).astype(F8)
    l8 = (lo * S_LO).astype(F8)
    for j, rows in enumerate(row_sets):
        part = slice(128 * j, 128 * j + 128)
        hi_ref[rows, 256 * n : 256 * n + 256] = hi[part]
        f8_ref[rows, 512 * n + 256 * flip : 512 * n + 256 * flip + 256] = h8[part]
        f8_ref[rows, 512 * n + 256 * (1 - flip) : 512 * n + 256 * (1 - flip) + 256] = l8[part]
        if lo_ref is not None:
            lo_ref[rows, 256 * n : 256 * n + 256] = lo[part].astype(BF16)


def lane_tile(g_ref, k, half):
    tiles = []
    for d in (4 * k + 2 * half, 4 * k + 2 * half + 1):
        tiles.append(jnp.concatenate([g_ref[d % 16, d // 16], jnp.zeros((5, 64), F32)], axis=0))
    return jnp.concatenate(tiles, axis=1)


def transposed(tile):
    return jnp.concatenate([tile, jnp.zeros((120, 128), F32)], axis=0).T


MESH = pl.DeviceIdType.MESH


def front_kernel(n_rows, n_cols, panel_ref, own_ref, l_ref, xcat, g_ref, m_ref, d_ref, row_buf, lt_buf, l_buf, pt, send_sem, recv_sem, local_sem):
    r = lax.axis_index("prow")
    c = lax.axis_index("pcol")
    local = pltpu.make_async_copy(own_ref, g_ref.at[c, r], local_sem)
    local.start()
    barrier = pltpu.get_barrier_semaphore()
    for i in range(1, n_rows):
        pl.semaphore_signal(barrier, inc=1, device_id=(lax.rem(r + i, n_rows), c), device_id_type=MESH)
    for i in range(1, n_cols):
        pl.semaphore_signal(barrier, inc=1, device_id=(r, lax.rem(c + i, n_cols)), device_id_type=MESH)

    def copy_to(src, dst, at, target):
        return pltpu.make_async_remote_copy(
            src_ref=src, dst_ref=dst, send_sem=send_sem.at[at], recv_sem=recv_sem.at[at], device_id=target, device_id_type=MESH
        )

    first = [copy_to(own_ref, g_ref.at[c, r], i, (lax.rem(r + i, n_rows), c)) for i in range(1, n_rows)]
    second = [copy_to(g_ref.at[c], g_ref.at[c], n_rows + i, (r, lax.rem(c + i, n_cols))) for i in range(1, n_cols)]

    def after(p):
        @pl.when(p == 0)
        def _():
            pl.semaphore_wait(barrier, n_rows + n_cols - 2)
            for copy in first:
                copy.start()

        @pl.when(p == 1)
        def _():
            local.wait()
            for copy in first:
                copy.wait()
            for copy in second:
                copy.start()

    for half in range(2):
        pt[128 * half : 128 * half + 128, :] = transposed(panel_ref[:, 128 * half : 128 * half + 128])
    chol(panel_ref, pt, m_ref, d_ref, row_buf, lt_buf, l_buf, xcat, after)
    l_ref[...] = l_buf[:768, :]
    for copy in second:
        copy.wait()


def front_call(panel8, own):
    n_rows, n_cols = lax.axis_size("prow"), lax.axis_size("pcol")
    vmem = pl.BlockSpec(memory_space=pltpu.VMEM)
    return pl.pallas_call(
        functools.partial(front_kernel, n_rows, n_cols),
        out_shape=[
            jax.ShapeDtypeStruct((768, 768), F32),
            jax.ShapeDtypeStruct((768, 2304), BF16),
            jax.ShapeDtypeStruct((n_cols, n_rows) + own.shape, F32),
        ],
        in_specs=[vmem, vmem],
        out_specs=[vmem, vmem, vmem],
        scratch_shapes=[
            pltpu.VMEM((1280, 1536), F32),
            pltpu.VMEM((128, 256), F32),
            pltpu.VMEM((128, 768), F32),
            pltpu.VMEM((640, 128), F32),
            pltpu.VMEM((1408, 768), F32),
            pltpu.VMEM((256, 128), F32),
            pltpu.SemaphoreType.DMA((n_rows + n_cols,)),
            pltpu.SemaphoreType.DMA((n_rows + n_cols,)),
            pltpu.SemaphoreType.DMA,
        ],
        compiler_params=pltpu.CompilerParams(collective_id=0, has_side_effects=True, vmem_limit_bytes=40 << 20),
        name="factor_and_gather",
    )(panel8, own)


def kernel(slot_ref, panel_ref, g_ref, xcat, own_ref, out_ref, chi, cf8, rhi0, rhi1, rf80, rf81, rlo, bcat, rowt, colt, colp, ids):
    step = pl.program_id(0)
    prow, pcol = ids()
    r_hi, r_f8 = (rhi0, rhi1), (rf80, rf81)

    def row_coords(tile):
        at = pl.multiple_of(tile * 128, 128)
        return lambda r, m: [rowt[pl.ds(at + r, m), k : k + 1] for k in range(3)]

    def rows_for(tile, which):
        panel_entries(row_coords(tile), panel_ref, bcat)
        for n in range(3):
            v = panel_dot(bcat, xcat, n)
            split_store(v, n, [slice(128 * j, 128 * j + 128) for j in range(3)], r_hi[which], r_f8[which], rlo, 0)

    def own_rows(tile, which):
        for h in range(3):
            piece = (pcol % 4) * 3 + h
            comp, quarter = piece // 4, piece % 4

            @pl.when((tile // 2 == pcol // 4) & (quarter // 2 == tile % 2))
            def _():
                at = pl.multiple_of(comp * 128 + (quarter % 2) * 64, 64)
                own_ref[64 * h : 64 * h + 64, :] = r_hi[which][pl.ds(at, 64), :].astype(F32) + rlo[pl.ds(at, 64), :].astype(F32)

    @pl.when(step == 0)
    def _():
        def rows_of(i, _):
            rowt[pl.ds(pl.multiple_of(i * 128, 128), 128), :] = transposed(lane_tile(g_ref, slot_ref[prow * 4 + i // 2], i % 2))
            return 0

        lax.fori_loop(0, 8, rows_of, 0)
        for i in range(4):
            tile = lane_tile(g_ref, slot_ref[pcol * 2 + i // 2], i % 2)
            colp[:, 128 * i : 128 * i + 128] = tile
            colt[128 * i : 128 * i + 128, :] = transposed(tile)

        def col_rows(i, _):
            at = pl.multiple_of(i * 128, 128)
            dst = (i // 2) * 768 + (i % 2) * 128
            panel_entries(lambda r, m: [colt[pl.ds(at + r, m), c : c + 1] for c in range(3)], panel_ref, bcat)
            for n in range(3):
                rows = [pl.ds(pl.multiple_of(dst + 256 * j, 128), 128) for j in range(3)]
                split_store(panel_dot(bcat, xcat, n), n, rows, chi, cf8, None, 1)
            return 0

        lax.fori_loop(0, 4, col_rows, 0)
        rows_for(0, 0)

    for which in range(2):
        tile = step * 2 + which
        coords = row_coords(tile)
        own_rows(tile, which)
        for c in range(2):
            for j in range(3):
                at = 768 * c + 256 * j
                v = lax.dot_general(r_hi[which][...], chi[at : at + 256, :], NT, preferred_element_type=F32)
                w = lax.dot_general(r_f8[which][...], cf8[at : at + 256, :], NT, preferred_element_type=F32)
                v = v + w * (1.0 / (S_HI * S_LO))
                out_ref[0, :, 128 * which : 128 * which + 128, at : at + 256] = v.reshape(3, 128, 256)
            for r in range(0, 128, 32):
                e = tensor_entries(coords(r, 32), [colp[k : k + 1, 256 * c : 256 * c + 256] for k in range(3)])
                for i in range(3):
                    for j in range(3):
                        dst = (0, i, slice(128 * which + r, 128 * which + r + 32), slice(768 * c + 256 * j, 768 * c + 256 * j + 256))
                        out_ref[dst] = e[i, j] - out_ref[dst]
        rows_for(jnp.minimum(tile + 1, 7), 1 - which)


def main_call(slot_block, panel8, gathered, xcat, ids):
    whole = lambda s: (0, 0)
    vmem = lambda shape, dtype: pltpu.VMEM(shape, dtype)
    own, out = pl.pallas_call(
        functools.partial(kernel, ids=ids),
        grid=(4,),
        in_specs=[
            pl.BlockSpec(memory_space=pltpu.SMEM),
            pl.BlockSpec((8, 256), whole),
            pl.BlockSpec((16, 8, 3, 64), lambda s: (0, 0, 0, 0)),
            pl.BlockSpec((768, 2304), whole),
        ],
        out_specs=[
            pl.BlockSpec((192, 768), whole),
            pl.BlockSpec((1, 3, 256, 1536), lambda s: (s, 0, 0, 0)),
        ],
        out_shape=[
            jax.ShapeDtypeStruct((192, 768), F32),
            jax.ShapeDtypeStruct((4, 3, 256, 1536), F32),
        ],
        scratch_shapes=[
            vmem((1536, 768), BF16),
            vmem((1536, 1536), F8),
            vmem((384, 768), BF16),
            vmem((384, 768), BF16),
            vmem((384, 1536), F8),
            vmem((384, 1536), F8),
            vmem((384, 768), BF16),
            vmem((384, 2304), BF16),
            vmem((1024, 128), F32),
            vmem((512, 128), F32),
            vmem((8, 512), F32),
        ],
        compiler_params=pltpu.CompilerParams(dimension_semantics=("arbitrary",), vmem_limit_bytes=40 << 20),
        name="panel_rows_and_trailing",
    )(slot_block, panel8, gathered, xcat)
    return own, out.reshape(3072, 1536)


def shards(panel_pos, trail_pos, slot_block):
    panel8 = jnp.pad(panel_pos, ((0, 5), (0, 0)))
    factor, xcat, gathered = front_call(panel8, trail_pos)
    own, trailing = main_call(slot_block, panel8, gathered, xcat, lambda: (lax.axis_index("prow"), lax.axis_index("pcol")))
    return factor, own, trailing


def solution(mesh):
    return jax.shard_map(
        shards,
        mesh=mesh,
        in_specs=(P(), P(None, ("prow", "pcol")), P()),
        out_specs=(P(), P(("prow", "pcol"), None), P("prow", "pcol")),
        check_vma=False,
    )
```

```python
import functools
import jax
import jax.numpy as jnp
from jax import lax
from jax.experimental import pallas as pl
from jax.experimental.pallas import tpu as pltpu
from jax.sharding import PartitionSpec as P

RADIUS = 0.25
F32, BF16, F8 = jnp.float32, jnp.bfloat16, jnp.float8_e4m3fn
NT = (((1,), (1,)), ((), ()))
NN = (((1,), (0,)), ((), ()))
TN = (((0,), (0,)), ((), ()))


def split(x):
    hi = x.astype(BF16)
    return hi, (x - hi.astype(F32)).astype(BF16)


def dot3(a, b, dims):
    ah, al = split(a)
    bh, bl = split(b)
    d = functools.partial(lax.dot_general, dimension_numbers=dims, preferred_element_type=F32)
    return d(ah, bh) + (d(al, bh) + d(ah, bl))


def pair_terms(rows, cols):
    diff = [r - c for r, c in zip(rows, cols)]
    squared = diff[0] * diff[0] + diff[1] * diff[1] + diff[2] * diff[2]
    same = squared < 0.01
    inv = lax.rsqrt(jnp.where(same, 1.0, squared))
    inv2 = inv * inv
    t = (0.75 * RADIUS) * inv
    t2 = t * inv2
    iso = jnp.where(same, 1.0, t + (RADIUS * RADIUS * 2.0 / 3.0) * t2)
    directed = t2 * (1.0 - (2.0 * RADIUS * RADIUS) * inv2)
    return diff, iso, directed


def tensor_entries(rows, cols):
    diff, iso, directed = pair_terms(rows, cols)
    g = [directed * d for d in diff]
    e = {}
    for i in range(3):
        for j in range(i, 3):
            v = g[i] * diff[j]
            if i == j:
                v = v + iso
            e[i, j] = e[j, i] = v
    return e


def bsub(row):
    return jnp.broadcast_to(row, (8, row.shape[-1]))


def rep(tile, rows):
    return jnp.concatenate([tile] * (rows // 8), axis=0)


def first_tile(tile, rest):
    return tile if rest.shape[0] == 8 else jnp.concatenate([tile, rest[8:]], axis=0)


def factor_block(d_ref):
    sub = lax.broadcasted_iota(jnp.int32, (8, 128), 0)
    a = d_ref[:, :128]
    inv = d_ref[:, 128:]
    for t in range(16):
        n = 128 - 8 * t
        cs = [jnp.broadcast_to(a[:, 8 * t + k : 8 * t + k + 1], (n, 128)) for k in range(8)]
        for j in range(8):
            rs = lax.rsqrt(bsub(cs[j][j : j + 1, :]))
            m = cs[j] * rep(rs, n)
            sp = [rep(bsub(m[k : k + 1, :]), n) for k in range(j + 1, 8)]
            m = first_tile(jnp.where(sub > j, m[:8], 0.0), m)
            ua = bsub(a[j : j + 1, :]) * rs
            ui = bsub(inv[j : j + 1, :]) * rs
            a = a - m * rep(ua, n)
            a = first_tile(jnp.where(sub == j, ua, a[:8]), a)
            inv = inv - m * rep(ui, n)
            inv = first_tile(jnp.where(sub == j, ui, inv[:8]), inv)
            for k in range(j + 1, 8):
                cs[k] = cs[k] - m * sp[k - j - 1]
        d_ref[8 * t : 8 * t + 8, :128] = a[:8]
        d_ref[8 * t : 8 * t + 8, 128:] = inv[:8]
        if t < 15:
            a, inv = a[8:], inv[8:]


def cat_store(ref, rows, chunk, hi, lo, order):
    base = 768 * chunk
    for i, w in enumerate(order):
        ref[rows, base + 256 * i : base + 256 * i + 256] = hi if w == "h" else lo


def pre_split_dot(a, b, dims):
    d = functools.partial(lax.dot_general, dimension_numbers=dims, preferred_element_type=F32)
    return d(a[0], b[0]) + (d(a[1], b[0]) + d(a[0], b[1]))


def chol(panel_ref, panel_t, m_ref, d_ref, row_buf, lt_buf, l_buf, xcat, after):
    m_ref[:768, 768:] = jnp.zeros((768, 768), F32)
    for r in range(0, 256, 32):
        rows = [panel_t[r : r + 32, c : c + 1] for c in range(3)]
        cols = [panel_ref[c : c + 1, :] for c in range(3)]
        e = tensor_entries(rows, cols)
        for i in range(3):
            for j in range(3):
                m_ref[256 * i + r : 256 * i + r + 32, 256 * j : 256 * j + 256] = e[i, j]
    rows_at = lax.broadcasted_iota(jnp.int32, (128, 128), 0)
    cols_at = lax.broadcasted_iota(jnp.int32, (128, 128), 1)
    eye = (rows_at == cols_at).astype(F32)
    l_buf[...] = jnp.zeros(l_buf.shape, F32)
    xcat[...] = jnp.zeros(xcat.shape, BF16)
    row_buf[...] = jnp.zeros(row_buf.shape, F32)
    lt_buf[...] = jnp.zeros(lt_buf.shape, F32)
    d_ref[:, :128] = m_ref[:128, :128]
    d_ref[:, 128:] = eye

    def panel(p, _):
        base = pl.multiple_of(128 * p, 128)
        nxt = pl.multiple_of(128 * p + 128, 128)
        for i in range(5):
            at = pl.multiple_of(base + 128 * i, 128)
            m_ref[pl.ds(at, 128), pl.ds(base, 768)] -= dot3(lt_buf[128 * i : 128 * i + 128, :], row_buf[...], NN)
        factor_block(d_ref)
        x = d_ref[:, 128:]
        l_buf[pl.ds(base, 128), pl.ds(base, 128)] = jnp.where(rows_at >= cols_at, d_ref[:, :128].T, 0.0)
        row = dot3(x, m_ref[pl.ds(base, 128), pl.ds(nxt, 640)], NN)
        row_buf[:, :640] = row
        row_buf[:, 640:] = x
        m_ref[pl.ds(base, 128), pl.ds(nxt, 640)] = row
        m_ref[pl.ds(base, 128), pl.ds(768 + base, 128)] = x
        first = row[:, :128].T
        d_ref[:, :128] = m_ref[pl.ds(nxt, 128), pl.ds(nxt, 128)] - dot3(first, row[:, :128], NN)
        d_ref[:, 128:] = eye
        lt_buf[:128, :] = first
        l_buf[pl.ds(nxt, 128), pl.ds(base, 128)] = first
        for i in range(1, 5):
            lt = row[:, 128 * i : 128 * i + 128].T
            lt_buf[128 * i : 128 * i + 128, :] = lt
            l_buf[pl.ds(pl.multiple_of(nxt + 128 * i, 128), 128), pl.ds(base, 128)] = lt
        after(p)
        return 0

    lax.fori_loop(0, 6, panel, 0)
    for k in range(3):
        hi, lo = split(m_ref[256 * k : 768, 768 + 256 * k : 1024 + 256 * k])
        cat_store(xcat, slice(256 * k, 768), k, hi, lo, "hhl")


def lane_tile(g_ref, k, half):
    tiles = []
    for d in (4 * k + 2 * half, 4 * k + 2 * half + 1):
        tiles.append(jnp.concatenate([g_ref[d % 16, d // 16], jnp.zeros((5, 64), F32)], axis=0))
    return jnp.concatenate(tiles, axis=1)


def transposed(tile):
    return jnp.concatenate([tile, jnp.zeros((120, 128), F32)], axis=0).T


MESH = pl.DeviceIdType.MESH


def front_kernel(n_rows, n_cols, panel_ref, own_ref, l_ref, xcat, g_ref, m_ref, d_ref, row_buf, lt_buf, l_buf, p8, pt, send_sem, recv_sem, local_sem):
    r = lax.axis_index("prow")
    c = lax.axis_index("pcol")
    local = pltpu.make_async_copy(own_ref, g_ref.at[c, r], local_sem)
    local.start()
    barrier = pltpu.get_barrier_semaphore()
    for i in range(1, n_rows):
        pl.semaphore_signal(barrier, inc=1, device_id=(lax.rem(r + i, n_rows), c), device_id_type=MESH)
    for i in range(1, n_cols):
        pl.semaphore_signal(barrier, inc=1, device_id=(r, lax.rem(c + i, n_cols)), device_id_type=MESH)

    def copy_to(src, dst, at, target):
        return pltpu.make_async_remote_copy(
            src_ref=src, dst_ref=dst, send_sem=send_sem.at[at], recv_sem=recv_sem.at[at], device_id=target, device_id_type=MESH
        )

    first = [copy_to(own_ref, g_ref.at[c, r], i, (lax.rem(r + i, n_rows), c)) for i in range(1, n_rows)]
    second = [copy_to(g_ref.at[c], g_ref.at[c], n_rows + i, (r, lax.rem(c + i, n_cols))) for i in range(1, n_cols)]

    def after(p):
        @pl.when(p == 0)
        def _():
            pl.semaphore_wait(barrier, n_rows + n_cols - 2)
            for copy in first:
                copy.start()

        @pl.when(p == 1)
        def _():
            local.wait()
            for copy in first:
                copy.wait()
            for copy in second:
                copy.start()

    p8[...] = jnp.zeros((8, 256), F32)
    p8[:3, :] = panel_ref[...]
    for half in range(2):
        pt[128 * half : 128 * half + 128, :] = transposed(p8[:, 128 * half : 128 * half + 128])
    chol(panel_ref, pt, m_ref, d_ref, row_buf, lt_buf, l_buf, xcat, after)
    l_ref[...] = l_buf[:768, :]
    for copy in second:
        copy.wait()


def front_call(panel_pos, own):
    n_rows, n_cols = lax.axis_size("prow"), lax.axis_size("pcol")
    vmem = pl.BlockSpec(memory_space=pltpu.VMEM)
    return pl.pallas_call(
        functools.partial(front_kernel, n_rows, n_cols),
        out_shape=[
            jax.ShapeDtypeStruct((768, 768), F32),
            jax.ShapeDtypeStruct((768, 2304), BF16),
            jax.ShapeDtypeStruct((n_cols, n_rows) + own.shape, F32),
        ],
        in_specs=[vmem, pl.BlockSpec(memory_space=pl.ANY)],
        out_specs=[vmem, vmem, vmem],
        cost_estimate=pl.CostEstimate(flops=10**10, bytes_accessed=10**7, transcendentals=0),
        scratch_shapes=[
            pltpu.VMEM((1280, 1536), F32),
            pltpu.VMEM((128, 256), F32),
            pltpu.VMEM((128, 768), F32),
            pltpu.VMEM((640, 128), F32),
            pltpu.VMEM((1408, 768), F32),
            pltpu.VMEM((8, 256), F32),
            pltpu.VMEM((256, 128), F32),
            pltpu.SemaphoreType.DMA((n_rows + n_cols,)),
            pltpu.SemaphoreType.DMA((n_rows + n_cols,)),
            pltpu.SemaphoreType.DMA,
        ],
        compiler_params=pltpu.CompilerParams(collective_id=0, has_side_effects=True, vmem_limit_bytes=40 << 20),
        name="factor_and_gather",
    )(panel_pos, own)


def panel_entries(rows, panel_ref, bcat):
    for r in range(0, 128, 32):
        e = tensor_entries(rows(r, 32), [panel_ref[c : c + 1, :] for c in range(3)])
        for i in range(3):
            for j in range(3):
                hi, lo = split(e[i, j])
                cat_store(bcat, slice(128 * i + r, 128 * i + r + 32), j, hi, lo, "hlh")


ROW = (2048.0, 256.0, 131072.0)
COL = (1024.0, 16.0, 8192.0)
BACK = 1.0 / (2048.0 * 1024.0)
F8_MAX = 448.0


def parts_of(v, scales):
    scaled = v * scales[0]
    hi = scaled.astype(BF16)
    rest = scaled - hi.astype(F32)
    return hi, scaled * (scales[1] / scales[0]), rest * (scales[2] / scales[0])


def row_parts(rows, panel_ref, hi_ref, f8_ref):
    for r in range(0, 128, 32):
        e = tensor_entries(rows(r, 32), [panel_ref[c : c + 1, :] for c in range(3)])
        parts = {(i, j): parts_of(e[i, j], ROW) for i in range(3) for j in range(i, 3)}
        for i in range(3):
            at = slice(128 * i + r, 128 * i + r + 32)
            for j in range(3):
                hi, whole, rest = parts[min(i, j), max(i, j)]
                hi_ref[at, 256 * j : 256 * j + 256] = hi
                f8_ref[at, 512 * j : 512 * j + 256] = whole.astype(F8)
                f8_ref[at, 512 * j + 256 : 512 * j + 512] = rest.astype(F8)


def col_store(v, dst, chi, cf8):
    for n in range(3):
        hi, whole, rest = parts_of(v[:, 256 * n : 256 * n + 256], COL)
        whole = jnp.clip(whole, -F8_MAX, F8_MAX).astype(F8)
        rest = jnp.clip(rest, -F8_MAX, F8_MAX).astype(F8)
        for j in range(3):
            rows, part = slice(dst + 256 * j, dst + 256 * j + 128), slice(128 * j, 128 * j + 128)
            chi[rows, 256 * n : 256 * n + 256] = hi[part]
            cf8[rows, 512 * n : 512 * n + 256] = rest[part]
            cf8[rows, 512 * n + 256 : 512 * n + 512] = whole[part]


def kernel(slot_ref, panel_ref, g_ref, xcat, l_in, l_out, own_ref, out_ref, wcat, chi, cf8, rhi, rf8, bcat, ocat, rowt, colt, colp, l_sem, ids):
    step = pl.program_id(0)
    prow, pcol = ids()
    l_copy = pltpu.make_async_copy(l_in, l_out, l_sem)
    panel_cols = lambda: [panel_ref[c : c + 1, :] for c in range(3)]

    def row_coords(tile):
        at = pl.multiple_of(tile * 128, 128)
        return lambda r, m: [rowt[pl.ds(at + r, m), k : k + 1] for k in range(3)]

    def inverse_of_diag():
        for b in range(3):
            for a in range(3):
                k = slice(256 * max(a, b), 768)
                hi = lambda q: xcat[k, 768 * q : 768 * q + 256]
                lo = lambda q: xcat[k, 768 * q + 512 : 768 * q + 768]
                w = pre_split_dot((hi(a), lo(a)), (hi(b), lo(b)), TN)
                wh, wl = split(w)
                at = slice(256 * b, 256 * b + 256)
                wcat[768 * a : 768 * a + 256, at] = wh
                wcat[768 * a + 256 : 768 * a + 512, at] = wh
                wcat[768 * a + 512 : 768 * a + 768, at] = wl

    def own_rows():
        for h in range(3):
            piece = (pcol % 4) * 3 + h
            comp, quarter = piece // 4, piece % 4
            at = pl.multiple_of((pcol // 4) * 256 + quarter * 64, 64)
            for r in range(0, 64, 32):
                diff, iso, directed = pair_terms([rowt[pl.ds(at + r, 32), k : k + 1] for k in range(3)], panel_cols())
                g = directed * jnp.where(comp == 0, diff[0], jnp.where(comp == 1, diff[1], diff[2]))
                for j in range(3):
                    hi, lo = split(g * diff[j] + jnp.where(comp == j, iso, 0.0))
                    cat_store(ocat, slice(64 * h + r, 64 * h + r + 32), j, hi, lo, "hlh")
        for n in range(3):
            k = 768 * (n + 1)
            own_ref[:, 256 * n : 256 * n + 256] = lax.dot_general(
                ocat[:, :k], xcat[256 * n : 256 * n + 256, :k], NT, preferred_element_type=F32
            )

    @pl.when(step == 0)
    def _():
        l_copy.start()

        def rows_of(i, _):
            rowt[pl.ds(pl.multiple_of(i * 128, 128), 128), :] = transposed(lane_tile(g_ref, slot_ref[prow * 4 + i // 2], i % 2))
            return 0

        lax.fori_loop(0, 8, rows_of, 0)
        for i in range(4):
            tile = lane_tile(g_ref, slot_ref[pcol * 2 + i // 2], i % 2)
            colp[:, 128 * i : 128 * i + 128] = tile
            colt[128 * i : 128 * i + 128, :] = transposed(tile)
        inverse_of_diag()
        for i in range(4):
            buf = bcat.at[i % 2]
            panel_entries(lambda r, m: [colt[128 * i + r : 128 * i + r + m, c : c + 1] for c in range(3)], panel_ref, buf)
            v = lax.dot_general(buf[...], wcat[...], NN, preferred_element_type=F32)
            col_store(v, (i // 2) * 768 + (i % 2) * 128, chi, cf8)
        own_rows()
        row_parts(row_coords(0), panel_ref, rhi.at[0], rf8.at[0])

    which = step % 2
    coords = row_coords(step)

    def trailing(c):
        at = 768 * c
        v = lax.dot_general(rhi[which], chi[at : at + 768, :], NT, preferred_element_type=F32)
        v = v + lax.dot_general(rf8[which], cf8[at : at + 768, :], NT, preferred_element_type=F32)
        out_ref[0, :, :, at : at + 768] = v.reshape(3, 128, 768)
        for r in range(0, 128, 32):
            e = tensor_entries(coords(r, 32), [colp[k : k + 1, 256 * c : 256 * c + 256] for k in range(3)])
            for i in range(3):
                for j in range(3):
                    dst = (0, i, slice(r, r + 32), slice(768 * c + 256 * j, 768 * c + 256 * j + 256))
                    out_ref[dst] = e[i, j] - out_ref[dst] * BACK

    @pl.when(step < 7)
    def _():
        trailing(0)
        row_parts(row_coords(step + 1), panel_ref, rhi.at[1 - which], rf8.at[1 - which])
        trailing(1)

    @pl.when(step == 7)
    def _():
        trailing(0)
        trailing(1)
        l_copy.wait()


def main_call(slot_block, panel_pos, gathered, xcat, factor, ids):
    whole = lambda s: (0, 0)
    vmem = lambda shape, dtype: pltpu.VMEM(shape, dtype)
    l, own, out = pl.pallas_call(
        functools.partial(kernel, ids=ids),
        grid=(8,),
        in_specs=[
            pl.BlockSpec(memory_space=pltpu.SMEM),
            pl.BlockSpec((3, 256), whole),
            pl.BlockSpec((16, 8, 3, 64), lambda s: (0, 0, 0, 0)),
            pl.BlockSpec((768, 2304), whole),
            pl.BlockSpec(memory_space=pltpu.VMEM),
        ],
        out_specs=[
            pl.BlockSpec(memory_space=pl.ANY),
            pl.BlockSpec((192, 768), whole),
            pl.BlockSpec((1, 3, 128, 1536), lambda s: (s // 2, 0, s % 2, 0)),
        ],
        out_shape=[
            jax.ShapeDtypeStruct((768, 768), F32),
            jax.ShapeDtypeStruct((192, 768), F32),
            jax.ShapeDtypeStruct((4, 3, 256, 1536), F32),
        ],
        scratch_shapes=[
            vmem((2304, 768), BF16),
            vmem((1536, 768), BF16),
            vmem((1536, 1536), F8),
            vmem((2, 384, 768), BF16),
            vmem((2, 384, 1536), F8),
            vmem((2, 384, 2304), BF16),
            vmem((192, 2304), BF16),
            vmem((1024, 128), F32),
            vmem((512, 128), F32),
            vmem((8, 512), F32),
            pltpu.SemaphoreType.DMA,
        ],
        compiler_params=pltpu.CompilerParams(dimension_semantics=("arbitrary",), vmem_limit_bytes=40 << 20),
        cost_estimate=pl.CostEstimate(flops=3 * 10**10, bytes_accessed=3 * 10**7, transcendentals=0),
        name="panel_rows_and_trailing",
    )(slot_block, panel_pos, gathered, xcat, factor)
    return l, own, out.reshape(3072, 1536)


def shards(panel_pos, trail_pos, slot_block):
    factor, xcat, gathered = front_call(panel_pos, trail_pos)
    return main_call(slot_block, panel_pos, gathered, xcat, factor, lambda: (lax.axis_index("prow"), lax.axis_index("pcol")))


def solution(mesh):
    return jax.shard_map(
        shards,
        mesh=mesh,
        in_specs=(P(), P(None, ("prow", "pcol")), P()),
        out_specs=(P(), P(("prow", "pcol"), None), P("prow", "pcol")),
        check_vma=False,
    )
```

```python
import functools
import jax
import jax.numpy as jnp
from jax import lax
from jax.experimental import pallas as pl
from jax.experimental.pallas import tpu as pltpu
from jax.sharding import PartitionSpec as P

RADIUS = 0.25
F32, BF16, F8 = jnp.float32, jnp.bfloat16, jnp.float8_e4m3fn
NT = (((1,), (1,)), ((), ()))
NN = (((1,), (0,)), ((), ()))
TN = (((0,), (0,)), ((), ()))


def split(x):
    hi = x.astype(BF16)
    return hi, (x - hi.astype(F32)).astype(BF16)


def dot3(a, b, dims):
    ah, al = split(a)
    bh, bl = split(b)
    d = functools.partial(lax.dot_general, dimension_numbers=dims, preferred_element_type=F32)
    return d(ah, bh) + (d(al, bh) + d(ah, bl))


def pair_terms(rows, cols):
    diff = [r - c for r, c in zip(rows, cols)]
    squared = diff[0] * diff[0] + diff[1] * diff[1] + diff[2] * diff[2]
    same = squared < 0.01
    inv = lax.rsqrt(jnp.where(same, 1.0, squared))
    inv2 = inv * inv
    t = (0.75 * RADIUS) * inv
    t2 = t * inv2
    iso = jnp.where(same, 1.0, t + (RADIUS * RADIUS * 2.0 / 3.0) * t2)
    directed = t2 * (1.0 - (2.0 * RADIUS * RADIUS) * inv2)
    return diff, iso, directed


def tensor_entries(rows, cols):
    diff, iso, directed = pair_terms(rows, cols)
    g = [directed * d for d in diff]
    e = {}
    for i in range(3):
        for j in range(i, 3):
            v = g[i] * diff[j]
            if i == j:
                v = v + iso
            e[i, j] = e[j, i] = v
    return e


def bsub(row):
    return jnp.broadcast_to(row, (8, row.shape[-1]))


def rep(tile, rows):
    return jnp.concatenate([tile] * (rows // 8), axis=0)


def first_tile(tile, rest):
    return tile if rest.shape[0] == 8 else jnp.concatenate([tile, rest[8:]], axis=0)


def factor_block(d_ref):
    sub = lax.broadcasted_iota(jnp.int32, (8, 128), 0)
    a = d_ref[:, :128]
    inv = d_ref[:, 128:]
    for t in range(16):
        n = 128 - 8 * t
        cs = [jnp.broadcast_to(a[:, 8 * t + k : 8 * t + k + 1], (n, 128)) for k in range(8)]
        for j in range(8):
            rs = lax.rsqrt(bsub(cs[j][j : j + 1, :]))
            m = cs[j] * rep(rs, n)
            sp = [rep(bsub(m[k : k + 1, :]), n) for k in range(j + 1, 8)]
            m = first_tile(jnp.where(sub > j, m[:8], 0.0), m)
            ua = bsub(a[j : j + 1, :]) * rs
            ui = bsub(inv[j : j + 1, :]) * rs
            a = a - m * rep(ua, n)
            a = first_tile(jnp.where(sub == j, ua, a[:8]), a)
            inv = inv - m * rep(ui, n)
            inv = first_tile(jnp.where(sub == j, ui, inv[:8]), inv)
            for k in range(j + 1, 8):
                cs[k] = cs[k] - m * sp[k - j - 1]
        d_ref[8 * t : 8 * t + 8, :128] = a[:8]
        d_ref[8 * t : 8 * t + 8, 128:] = inv[:8]
        if t < 15:
            a, inv = a[8:], inv[8:]


def cat_store(ref, rows, chunk, hi, lo, order):
    base = 768 * chunk
    for i, w in enumerate(order):
        ref[rows, base + 256 * i : base + 256 * i + 256] = hi if w == "h" else lo


def pre_split_dot(a, b, dims):
    d = functools.partial(lax.dot_general, dimension_numbers=dims, preferred_element_type=F32)
    return d(a[0], b[0]) + (d(a[1], b[0]) + d(a[0], b[1]))


def chol(panel_ref, panel_t, m_ref, d_ref, row_buf, lt_buf, l_buf, xcat, after):
    m_ref[128:768, 768:1408] = jnp.zeros((640, 640), F32)
    for r in range(0, 256, 32):
        rows = [panel_t[r : r + 32, c : c + 1] for c in range(3)]
        cols = [panel_ref[c : c + 1, :] for c in range(3)]
        e = tensor_entries(rows, cols)
        for i in range(3):
            for j in range(3):
                m_ref[256 * i + r : 256 * i + r + 32, 256 * j : 256 * j + 256] = e[i, j]
    rows_at = lax.broadcasted_iota(jnp.int32, (128, 128), 0)
    cols_at = lax.broadcasted_iota(jnp.int32, (128, 128), 1)
    eye = (rows_at == cols_at).astype(F32)
    row_buf[...] = jnp.zeros(row_buf.shape, F32)
    lt_buf[...] = jnp.zeros(lt_buf.shape, F32)
    d_ref[:, :128] = m_ref[:128, :128]
    d_ref[:, 128:] = eye

    def panel(p, _):
        base = pl.multiple_of(128 * p, 128)
        nxt = pl.multiple_of(128 * p + 128, 128)
        row_parts = split(row_buf[...])
        for i in range(5):
            at = pl.multiple_of(base + 128 * i, 128)
            lt_parts = split(lt_buf[128 * i : 128 * i + 128, :])
            m_ref[pl.ds(at, 128), pl.ds(base, 768)] -= pre_split_dot(lt_parts, row_parts, NN)
        factor_block(d_ref)
        x = d_ref[:, 128:]
        l_buf[pl.ds(base, 128), pl.ds(base, 128)] = jnp.where(rows_at >= cols_at, d_ref[:, :128].T, 0.0)
        row = dot3(x, m_ref[pl.ds(base, 128), pl.ds(nxt, 640)], NN)
        row_buf[:, :640] = row
        row_buf[:, 640:] = x
        m_ref[pl.ds(base, 128), pl.ds(nxt, 640)] = row
        m_ref[pl.ds(base, 128), pl.ds(768 + base, 128)] = x
        first = row[:, :128].T
        d_ref[:, :128] = m_ref[pl.ds(nxt, 128), pl.ds(nxt, 128)] - dot3(first, row[:, :128], NN)
        d_ref[:, 128:] = eye
        lt_buf[:128, :] = first
        l_buf[pl.ds(nxt, 128), pl.ds(base, 128)] = first
        for i in range(1, 5):
            lt = row[:, 128 * i : 128 * i + 128].T
            lt_buf[128 * i : 128 * i + 128, :] = lt
            l_buf[pl.ds(pl.multiple_of(nxt + 128 * i, 128), 128), pl.ds(base, 128)] = lt
        after(p)
        return 0

    lax.fori_loop(0, 6, panel, 0)
    for q in range(6):
        rows = slice(128 * q, 128 * q + 128)
        for c in range(6):
            zero = jnp.zeros((128, 128), BF16)
            hi, lo = (zero, zero) if c > q else split(m_ref[rows, 768 + 128 * c : 896 + 128 * c])
            at = 768 * (c // 2) + 128 * (c % 2)
            xcat[rows, at : at + 128] = hi
            xcat[rows, at + 256 : at + 384] = hi
            xcat[rows, at + 512 : at + 640] = lo


def store_factor(l_ref, l_buf):
    for q in range(6):
        rows = slice(128 * q, 128 * q + 128)
        l_ref[rows, : 128 * q + 128] = l_buf[rows, : 128 * q + 128]
        if q < 5:
            l_ref[rows, 128 * q + 128 :] = jnp.zeros((128, 640 - 128 * q), F32)


def lane_tile(g_ref, k, half):
    tiles = []
    for d in (4 * k + 2 * half, 4 * k + 2 * half + 1):
        tiles.append(jnp.concatenate([g_ref[d % 16, d // 16], jnp.zeros((5, 64), F32)], axis=0))
    return jnp.concatenate(tiles, axis=1)


def transposed(tile):
    return jnp.concatenate([tile, jnp.zeros((120, 128), F32)], axis=0).T


MESH = pl.DeviceIdType.MESH


def front_kernel(n_rows, n_cols, panel_ref, own_ref, l_ref, xcat, g_ref, p8, m_ref, d_ref, row_buf, lt_buf, l_buf, p3, pt, send_sem, recv_sem, local_sem, panel_sem):
    r = lax.axis_index("prow")
    c = lax.axis_index("pcol")
    local = pltpu.make_async_copy(own_ref, g_ref.at[c, r], local_sem)
    local.start()
    panel_copy = pltpu.make_async_copy(panel_ref, p3, panel_sem)
    panel_copy.start()
    barrier = pltpu.get_barrier_semaphore()
    for i in range(1, n_rows):
        pl.semaphore_signal(barrier, inc=1, device_id=(lax.rem(r + i, n_rows), c), device_id_type=MESH)
    for i in range(1, n_cols):
        pl.semaphore_signal(barrier, inc=1, device_id=(r, lax.rem(c + i, n_cols)), device_id_type=MESH)

    def copy_to(src, dst, at, target):
        return pltpu.make_async_remote_copy(
            src_ref=src, dst_ref=dst, send_sem=send_sem.at[at], recv_sem=recv_sem.at[at], device_id=target, device_id_type=MESH
        )

    first = [copy_to(own_ref, g_ref.at[c, r], i, (lax.rem(r + i, n_rows), c)) for i in range(1, n_rows)]
    second = [copy_to(g_ref.at[c], g_ref.at[c], n_rows + i, (r, lax.rem(c + i, n_cols))) for i in range(1, n_cols)]

    def after(p):
        @pl.when(p == 0)
        def _():
            pl.semaphore_wait(barrier, n_rows + n_cols - 2)
            for copy in first:
                copy.start()

        @pl.when(p == 1)
        def _():
            local.wait()
            for copy in first:
                copy.wait()
            for copy in second:
                copy.start()

    p8[...] = jnp.zeros((8, 256), F32)
    panel_copy.wait()
    p8[:3, :] = p3[...]
    for half in range(2):
        pt[128 * half : 128 * half + 128, :] = transposed(p8[:, 128 * half : 128 * half + 128])
    chol(p8, pt, m_ref, d_ref, row_buf, lt_buf, l_buf, xcat, after)
    store_factor(l_ref, l_buf)
    for copy in second:
        copy.wait()


def front_call(panel_pos, own):
    n_rows, n_cols = lax.axis_size("prow"), lax.axis_size("pcol")
    vmem = pl.BlockSpec(memory_space=pltpu.VMEM)
    return pl.pallas_call(
        functools.partial(front_kernel, n_rows, n_cols),
        out_shape=[
            jax.ShapeDtypeStruct((768, 768), F32),
            jax.ShapeDtypeStruct((768, 2304), BF16),
            jax.ShapeDtypeStruct((n_cols, n_rows) + own.shape, F32),
            jax.ShapeDtypeStruct((8, 256), F32),
        ],
        in_specs=[pl.BlockSpec(memory_space=pltpu.HBM)] * 2,
        out_specs=[vmem] * 4,
        cost_estimate=pl.CostEstimate(flops=10**10, bytes_accessed=10**7, transcendentals=0),
        scratch_shapes=[
            pltpu.VMEM((1280, 1536), F32),
            pltpu.VMEM((128, 256), F32),
            pltpu.VMEM((128, 768), F32),
            pltpu.VMEM((640, 128), F32),
            pltpu.VMEM((1408, 768), F32),
            pltpu.VMEM((3, 256), F32),
            pltpu.VMEM((256, 128), F32),
            pltpu.SemaphoreType.DMA((n_rows + n_cols,)),
            pltpu.SemaphoreType.DMA((n_rows + n_cols,)),
            pltpu.SemaphoreType.DMA,
            pltpu.SemaphoreType.DMA,
        ],
        compiler_params=pltpu.CompilerParams(collective_id=0, has_side_effects=True, vmem_limit_bytes=40 << 20),
        name="factor_and_gather",
    )(panel_pos, own)


def panel_entries(rows, panel_ref, bcat):
    for r in range(0, 128, 32):
        e = tensor_entries(rows(r, 32), [panel_ref[c : c + 1, :] for c in range(3)])
        for i in range(3):
            for j in range(3):
                hi, lo = split(e[i, j])
                cat_store(bcat, slice(128 * i + r, 128 * i + r + 32), j, hi, lo, "hlh")


ROW = (2048.0, 256.0, 131072.0)
COL = (1024.0, 16.0, 8192.0)
BACK = 1.0 / (2048.0 * 1024.0)
F8_MAX = 448.0


def parts_of(v, scales):
    scaled = v * scales[0]
    hi = scaled.astype(BF16)
    rest = scaled - hi.astype(F32)
    return hi, scaled * (scales[1] / scales[0]), rest * (scales[2] / scales[0])


def row_parts(rows, panel_ref, hi_ref, f8_ref):
    for r in range(0, 128, 32):
        e = tensor_entries(rows(r, 32), [panel_ref[c : c + 1, :] for c in range(3)])
        parts = {(i, j): parts_of(e[i, j], ROW) for i in range(3) for j in range(i, 3)}
        for i in range(3):
            at = slice(128 * i + r, 128 * i + r + 32)
            for j in range(3):
                hi, whole, rest = parts[min(i, j), max(i, j)]
                hi_ref[at, 256 * j : 256 * j + 256] = hi
                f8_ref[at, 512 * j : 512 * j + 256] = whole.astype(F8)
                f8_ref[at, 512 * j + 256 : 512 * j + 512] = rest.astype(F8)


def col_store(v, dst, chi, cf8):
    for n in range(3):
        hi, whole, rest = parts_of(v[:, 256 * n : 256 * n + 256], COL)
        whole = jnp.clip(whole, -F8_MAX, F8_MAX).astype(F8)
        rest = jnp.clip(rest, -F8_MAX, F8_MAX).astype(F8)
        for j in range(3):
            rows, part = slice(dst + 256 * j, dst + 256 * j + 128), slice(128 * j, 128 * j + 128)
            chi[rows, 256 * n : 256 * n + 256] = hi[part]
            cf8[rows, 512 * n : 512 * n + 256] = rest[part]
            cf8[rows, 512 * n + 256 : 512 * n + 512] = whole[part]


def kernel(slot_ref, panel_ref, g_ref, xcat, l_in, l_out, own_out, out_ref, own_ref, wcat, chi, cf8, rhi0, rhi1, rf80, rf81, bcat, ocat, rowt, colt, colp, obuf, l_sem, own_sem, o_sem, ids):
    prow, pcol = ids()
    l_copy = pltpu.make_async_copy(l_in, l_out, l_sem)
    own_copy = pltpu.make_async_copy(own_ref, own_out, own_sem)
    l_copy.start()

    def out_copy(at_step, half):
        rows = pl.ds(128 * half, 128)
        return pltpu.make_async_copy(obuf.at[at_step % 2, half], out_ref.at[at_step, :, rows, :], o_sem.at[at_step % 2, half])

    panel_cols = lambda: [panel_ref[c : c + 1, :] for c in range(3)]

    def row_coords(tile):
        at = pl.multiple_of(tile * 128, 128)
        return lambda r, m: [rowt[pl.ds(at + r, m), k : k + 1] for k in range(3)]

    def inverse_of_diag():
        for b in range(3):
            for a in range(3):
                k = slice(256 * max(a, b), 768)
                hi = lambda q: xcat[k, 768 * q : 768 * q + 256]
                lo = lambda q: xcat[k, 768 * q + 512 : 768 * q + 768]
                w = pre_split_dot((hi(a), lo(a)), (hi(b), lo(b)), TN)
                wh, wl = split(w)
                at = slice(256 * b, 256 * b + 256)
                wcat[768 * a : 768 * a + 256, at] = wh
                wcat[768 * a + 256 : 768 * a + 512, at] = wh
                wcat[768 * a + 512 : 768 * a + 768, at] = wl

    def own_rows():
        for h in range(3):
            piece = (pcol % 4) * 3 + h
            comp, quarter = piece // 4, piece % 4
            at = pl.multiple_of((pcol // 4) * 256 + quarter * 64, 64)
            for r in range(0, 64, 32):
                diff, iso, directed = pair_terms([rowt[pl.ds(at + r, 32), k : k + 1] for k in range(3)], panel_cols())
                g = directed * jnp.where(comp == 0, diff[0], jnp.where(comp == 1, diff[1], diff[2]))
                for j in range(3):
                    hi, lo = split(g * diff[j] + jnp.where(comp == j, iso, 0.0))
                    cat_store(ocat, slice(64 * h + r, 64 * h + r + 32), j, hi, lo, "hlh")
        for n in range(3):
            k = 768 * (n + 1)
            own_ref[:, 256 * n : 256 * n + 256] = lax.dot_general(
                ocat[:, :k], xcat[256 * n : 256 * n + 256, :k], NT, preferred_element_type=F32
            )

    def rows_of(i, _):
        rowt[pl.ds(pl.multiple_of(i * 128, 128), 128), :] = transposed(lane_tile(g_ref, slot_ref[prow * 4 + i // 2], i % 2))
        return 0

    lax.fori_loop(0, 8, rows_of, 0)
    for i in range(4):
        tile = lane_tile(g_ref, slot_ref[pcol * 2 + i // 2], i % 2)
        colp[:, 128 * i : 128 * i + 128] = tile
        colt[128 * i : 128 * i + 128, :] = transposed(tile)
    inverse_of_diag()
    for i in range(4):
        buf = bcat.at[i % 2]
        panel_entries(lambda r, m: [colt[128 * i + r : 128 * i + r + m, c : c + 1] for c in range(3)], panel_ref, buf)
        v = lax.dot_general(buf[...], wcat[...], NN, preferred_element_type=F32)
        col_store(v, (i // 2) * 768 + (i % 2) * 128, chi, cf8)
    own_rows()
    own_copy.start()
    row_parts(row_coords(0), panel_ref, rhi0, rf80)

    def trailing(step, slot, which, c):
        coords = row_coords(2 * step + which)
        at = 768 * c
        v = lax.dot_general((rhi0, rhi1)[which][...], chi[at : at + 768, :], NT, preferred_element_type=F32)
        v = v + lax.dot_general((rf80, rf81)[which][...], cf8[at : at + 768, :], NT, preferred_element_type=F32)
        obuf[slot, which, :, :, at : at + 768] = v.reshape(3, 128, 768)
        for r in range(0, 128, 32):
            e = tensor_entries(coords(r, 32), [colp[k : k + 1, 256 * c : 256 * c + 256] for k in range(3)])
            for i in range(3):
                for j in range(3):
                    dst = (slot, which, i, slice(r, r + 32), slice(768 * c + 256 * j, 768 * c + 256 * j + 256))
                    obuf[dst] = e[i, j] - obuf[dst] * BACK

    def two_tiles(step, _):
        slot = step % 2

        @pl.when(step >= 2)
        def _():
            for half in range(2):
                out_copy(step - 2, half).wait()

        trailing(step, slot, 0, 0)
        row_parts(row_coords(2 * step + 1), panel_ref, rhi1, rf81)
        trailing(step, slot, 0, 1)
        out_copy(step, 0).start()
        trailing(step, slot, 1, 0)
        row_parts(row_coords(jnp.minimum(2 * step + 2, 7)), panel_ref, rhi0, rf80)
        trailing(step, slot, 1, 1)
        out_copy(step, 1).start()
        return 0

    lax.fori_loop(0, 4, two_tiles, 0)
    for step in (2, 3):
        for half in range(2):
            out_copy(step, half).wait()
    own_copy.wait()
    l_copy.wait()


def main_call(slot_block, panel_pos, gathered, xcat, factor, ids):
    whole = pl.BlockSpec(memory_space=pltpu.VMEM)
    anywhere = pl.BlockSpec(memory_space=pl.ANY)
    vmem = lambda shape, dtype: pltpu.VMEM(shape, dtype)
    l, own, out = pl.pallas_call(
        functools.partial(kernel, ids=ids),
        in_specs=[pl.BlockSpec(memory_space=pltpu.SMEM), whole, whole, whole, whole],
        out_specs=[anywhere] * 3,
        out_shape=[
            jax.ShapeDtypeStruct((768, 768), F32),
            jax.ShapeDtypeStruct((192, 768), F32),
            jax.ShapeDtypeStruct((4, 3, 256, 1536), F32),
        ],
        scratch_shapes=[
            vmem((192, 768), F32),
            vmem((2304, 768), BF16),
            vmem((1536, 768), BF16),
            vmem((1536, 1536), F8),
            vmem((384, 768), BF16),
            vmem((384, 768), BF16),
            vmem((384, 1536), F8),
            vmem((384, 1536), F8),
            vmem((2, 384, 2304), BF16),
            vmem((192, 2304), BF16),
            vmem((1024, 128), F32),
            vmem((512, 128), F32),
            vmem((8, 512), F32),
            vmem((2, 2, 3, 128, 1536), F32),
            pltpu.SemaphoreType.DMA,
            pltpu.SemaphoreType.DMA,
            pltpu.SemaphoreType.DMA((2, 2)),
        ],
        compiler_params=pltpu.CompilerParams(vmem_limit_bytes=40 << 20),
        cost_estimate=pl.CostEstimate(flops=3 * 10**10, bytes_accessed=3 * 10**7, transcendentals=0),
        name="panel_rows_and_trailing",
    )(slot_block, panel_pos, gathered, xcat, factor)
    return l, own, out.reshape(3072, 1536)


def shards(panel_pos, trail_pos, slot_block):
    factor, xcat, gathered, panel8 = front_call(panel_pos, trail_pos)
    return main_call(slot_block, panel8, gathered, xcat, factor, lambda: (lax.axis_index("prow"), lax.axis_index("pcol")))


def solution(mesh):
    return jax.shard_map(
        shards,
        mesh=mesh,
        in_specs=(P(), P(None, ("prow", "pcol")), P()),
        out_specs=(P(), P(("prow", "pcol"), None), P("prow", "pcol")),
        check_vma=False,
    )
```

```python
import functools
import jax
import jax.numpy as jnp
from jax import lax
from jax.experimental import pallas as pl
from jax.experimental.pallas import tpu as pltpu
from jax.sharding import PartitionSpec as P

RADIUS = 0.25
F32, BF16, F8 = jnp.float32, jnp.bfloat16, jnp.float8_e4m3fn
NT = (((1,), (1,)), ((), ()))
NN = (((1,), (0,)), ((), ()))
TN = (((0,), (0,)), ((), ()))


def split(x):
    hi = x.astype(BF16)
    return hi, (x - hi.astype(F32)).astype(BF16)


def dot3(a, b, dims):
    ah, al = split(a)
    bh, bl = split(b)
    d = functools.partial(lax.dot_general, dimension_numbers=dims, preferred_element_type=F32)
    return d(ah, bh) + (d(al, bh) + d(ah, bl))


def pair_terms(rows, cols):
    diff = [r - c for r, c in zip(rows, cols)]
    squared = diff[0] * diff[0] + diff[1] * diff[1] + diff[2] * diff[2]
    same = squared < 0.01
    inv = lax.rsqrt(jnp.where(same, 1.0, squared))
    inv2 = inv * inv
    t = (0.75 * RADIUS) * inv
    t2 = t * inv2
    iso = jnp.where(same, 1.0, t + (RADIUS * RADIUS * 2.0 / 3.0) * t2)
    directed = t2 * (1.0 - (2.0 * RADIUS * RADIUS) * inv2)
    return diff, iso, directed


def tensor_entries(rows, cols):
    diff, iso, directed = pair_terms(rows, cols)
    g = [directed * d for d in diff]
    e = {}
    for i in range(3):
        for j in range(i, 3):
            v = g[i] * diff[j]
            if i == j:
                v = v + iso
            e[i, j] = e[j, i] = v
    return e


def bsub(row):
    return jnp.broadcast_to(row, (8, row.shape[-1]))


def rep(tile, rows):
    return jnp.concatenate([tile] * (rows // 8), axis=0)


def first_tile(tile, rest):
    return tile if rest.shape[0] == 8 else jnp.concatenate([tile, rest[8:]], axis=0)


def factor_block(d_ref):
    sub = lax.broadcasted_iota(jnp.int32, (8, 128), 0)
    a = d_ref[:, :128]
    inv = d_ref[:, 128:]
    for t in range(16):
        n = 128 - 8 * t
        cs = [jnp.broadcast_to(a[:, 8 * t + k : 8 * t + k + 1], (n, 128)) for k in range(8)]
        for j in range(8):
            rs = lax.rsqrt(bsub(cs[j][j : j + 1, :]))
            m = cs[j] * rep(rs, n)
            sp = [rep(bsub(m[k : k + 1, :]), n) for k in range(j + 1, 8)]
            m = first_tile(jnp.where(sub > j, m[:8], 0.0), m)
            ua = bsub(a[j : j + 1, :]) * rs
            ui = bsub(inv[j : j + 1, :]) * rs
            a = a - m * rep(ua, n)
            a = first_tile(jnp.where(sub == j, ua, a[:8]), a)
            inv = inv - m * rep(ui, n)
            inv = first_tile(jnp.where(sub == j, ui, inv[:8]), inv)
            for k in range(j + 1, 8):
                cs[k] = cs[k] - m * sp[k - j - 1]
        d_ref[8 * t : 8 * t + 8, :128] = a[:8]
        d_ref[8 * t : 8 * t + 8, 128:] = inv[:8]
        if t < 15:
            a, inv = a[8:], inv[8:]


def cat_store(ref, rows, chunk, hi, lo, order):
    base = 768 * chunk
    for i, w in enumerate(order):
        ref[rows, base + 256 * i : base + 256 * i + 256] = hi if w == "h" else lo


def pre_split_dot(a, b, dims):
    d = functools.partial(lax.dot_general, dimension_numbers=dims, preferred_element_type=F32)
    return d(a[0], b[0]) + (d(a[1], b[0]) + d(a[0], b[1]))


def chol(panel_ref, panel_t, m_ref, d_ref, row_buf, lt_buf, l_buf, xcat, after):
    m_ref[128:768, 768:1408] = jnp.zeros((640, 640), F32)
    for r in range(0, 256, 32):
        rows = [panel_t[r : r + 32, c : c + 1] for c in range(3)]
        cols = [panel_ref[c : c + 1, :] for c in range(3)]
        e = tensor_entries(rows, cols)
        for i in range(3):
            for j in range(3):
                m_ref[256 * i + r : 256 * i + r + 32, 256 * j : 256 * j + 256] = e[i, j]
    rows_at = lax.broadcasted_iota(jnp.int32, (128, 128), 0)
    cols_at = lax.broadcasted_iota(jnp.int32, (128, 128), 1)
    eye = (rows_at == cols_at).astype(F32)
    row_buf[...] = jnp.zeros(row_buf.shape, F32)
    lt_buf[...] = jnp.zeros(lt_buf.shape, F32)
    d_ref[:, :128] = m_ref[:128, :128]
    d_ref[:, 128:] = eye

    def panel(p, _):
        base = pl.multiple_of(128 * p, 128)
        nxt = pl.multiple_of(128 * p + 128, 128)
        row_parts = split(row_buf[...])
        for i in range(5):
            at = pl.multiple_of(base + 128 * i, 128)
            lt_parts = split(lt_buf[128 * i : 128 * i + 128, :])
            m_ref[pl.ds(at, 128), pl.ds(base, 768)] -= pre_split_dot(lt_parts, row_parts, NN)
        factor_block(d_ref)
        x = d_ref[:, 128:]
        l_buf[pl.ds(base, 128), pl.ds(base, 128)] = jnp.where(rows_at >= cols_at, d_ref[:, :128].T, 0.0)
        row = dot3(x, m_ref[pl.ds(base, 128), pl.ds(nxt, 640)], NN)
        row_buf[:, :640] = row
        row_buf[:, 640:] = x
        m_ref[pl.ds(base, 128), pl.ds(nxt, 640)] = row
        m_ref[pl.ds(base, 128), pl.ds(768 + base, 128)] = x
        first = row[:, :128].T
        d_ref[:, :128] = m_ref[pl.ds(nxt, 128), pl.ds(nxt, 128)] - dot3(first, row[:, :128], NN)
        d_ref[:, 128:] = eye
        lt_buf[:128, :] = first
        l_buf[pl.ds(nxt, 128), pl.ds(base, 128)] = first
        for i in range(1, 5):
            lt = row[:, 128 * i : 128 * i + 128].T
            lt_buf[128 * i : 128 * i + 128, :] = lt
            l_buf[pl.ds(pl.multiple_of(nxt + 128 * i, 128), 128), pl.ds(base, 128)] = lt
        after(p)
        return 0

    lax.fori_loop(0, 6, panel, 0)
    for q in range(6):
        rows = slice(128 * q, 128 * q + 128)
        for c in range(6):
            zero = jnp.zeros((128, 128), BF16)
            hi, lo = (zero, zero) if c > q else split(m_ref[rows, 768 + 128 * c : 896 + 128 * c])
            at = 768 * (c // 2) + 128 * (c % 2)
            xcat[rows, at : at + 128] = hi
            xcat[rows, at + 256 : at + 384] = hi
            xcat[rows, at + 512 : at + 640] = lo


def store_factor(l_ref, l_buf):
    for q in range(6):
        rows = slice(128 * q, 128 * q + 128)
        l_ref[rows, : 128 * q + 128] = l_buf[rows, : 128 * q + 128]
        if q < 5:
            l_ref[rows, 128 * q + 128 :] = jnp.zeros((128, 640 - 128 * q), F32)


def lane_tile(g_ref, k, half):
    tiles = []
    for d in (4 * k + 2 * half, 4 * k + 2 * half + 1):
        tiles.append(jnp.concatenate([g_ref[d % 16, d // 16][:, :64], jnp.zeros((5, 64), F32)], axis=0))
    return jnp.concatenate(tiles, axis=1)


def transposed(tile):
    return jnp.concatenate([tile, jnp.zeros((120, 128), F32)], axis=0).T


MESH = pl.DeviceIdType.MESH


def front_kernel(x_ref, l_ref, xcat, g_ref, p8, m_ref, d_ref, row_buf, lt_buf, l_buf, pt, send_sem, recv_sem, local_sem):
    r = lax.axis_index("prow")
    c = lax.axis_index("pcol")
    core, z, y, x = r % 2, r // 2, c % 4, c // 4
    own_ref = x_ref.at[:, 256:384]
    local = pltpu.make_async_copy(own_ref, g_ref.at[c, r], local_sem)
    local.start()
    pair, line, plane = g_ref.at[c, pl.ds(2 * z, 2)], g_ref.at[c], g_ref.at[pl.ds(4 * x, 4)]
    plan = [
        [(own_ref, g_ref.at[c, r], (r + 1 - 2 * core, c))],
        [(pair, pair, (lax.rem(z + i, 4) * 2 + core, c)) for i in range(1, 4)],
        [(line, line, (r, x * 4 + lax.rem(y + i, 4))) for i in range(1, 4)],
        [(plane, plane, (r, lax.rem(x + i, 4) * 4 + y)) for i in range(1, 4)],
    ]
    barrier = pltpu.get_barrier_semaphore()
    for stage in plan:
        for _, _, target in stage:
            pl.semaphore_signal(barrier, inc=1, device_id=target, device_id_type=MESH)

    stages = []
    for k, stage in enumerate(plan):
        stages.append([
            pltpu.make_async_remote_copy(
                src_ref=src,
                dst_ref=dst,
                send_sem=send_sem.at[3 * k + i],
                recv_sem=recv_sem.at[3 * k + i],
                device_id=target,
                device_id_type=MESH,
            )
            for i, (src, dst, target) in enumerate(stage)
        ])

    def after(p):
        @pl.when(p == 0)
        def _():
            pl.semaphore_wait(barrier, 10)
            for copy in stages[0]:
                copy.start()

        for k in range(1, 4):

            @pl.when(p == k)
            def _():
                if k == 1:
                    local.wait()
                for copy in stages[k - 1]:
                    copy.wait()
                for copy in stages[k]:
                    copy.start()

    p8[...] = jnp.zeros((8, 256), F32)
    p8[:3, :] = x_ref[:, :256]
    for half in range(2):
        pt[128 * half : 128 * half + 128, :] = transposed(p8[:, 128 * half : 128 * half + 128])
    chol(p8, pt, m_ref, d_ref, row_buf, lt_buf, l_buf, xcat, after)
    store_factor(l_ref, l_buf)
    for copy in stages[3]:
        copy.wait()


def front_call(panel_pos, own):
    vmem = pl.BlockSpec(memory_space=pltpu.VMEM)
    together = jnp.concatenate([panel_pos, jnp.pad(own, ((0, 0), (0, 128 - own.shape[1])))], axis=1)
    return pl.pallas_call(
        front_kernel,
        out_shape=[
            jax.ShapeDtypeStruct((768, 768), F32),
            jax.ShapeDtypeStruct((768, 2304), BF16),
            jax.ShapeDtypeStruct((16, 8, 3, 128), F32),
            jax.ShapeDtypeStruct((8, 256), F32),
        ],
        in_specs=[vmem],
        out_specs=[vmem] * 4,
        cost_estimate=pl.CostEstimate(flops=10**10, bytes_accessed=10**7, transcendentals=0),
        scratch_shapes=[
            pltpu.VMEM((1280, 1536), F32),
            pltpu.VMEM((128, 256), F32),
            pltpu.VMEM((128, 768), F32),
            pltpu.VMEM((640, 128), F32),
            pltpu.VMEM((1408, 768), F32),
            pltpu.VMEM((256, 128), F32),
            pltpu.SemaphoreType.DMA((12,)),
            pltpu.SemaphoreType.DMA((12,)),
            pltpu.SemaphoreType.DMA,
        ],
        compiler_params=pltpu.CompilerParams(collective_id=0, has_side_effects=True, vmem_limit_bytes=40 << 20),
        name="factor_and_gather",
    )(together)


def panel_entries(rows, panel_ref, bcat):
    for r in range(0, 128, 32):
        e = tensor_entries(rows(r, 32), [panel_ref[c : c + 1, :] for c in range(3)])
        for i in range(3):
            for j in range(3):
                hi, lo = split(e[i, j])
                cat_store(bcat, slice(128 * i + r, 128 * i + r + 32), j, hi, lo, "hlh")


ROW = (2048.0, 256.0, 131072.0)
COL = (1024.0, 16.0, 8192.0)
BACK = 1.0 / (2048.0 * 1024.0)
F8_MAX = 448.0


def parts_of(v, scales):
    scaled = v * scales[0]
    hi = scaled.astype(BF16)
    rest = scaled - hi.astype(F32)
    return hi, scaled * (scales[1] / scales[0]), rest * (scales[2] / scales[0])


def row_parts(rows, panel_ref, hi_ref, f8_ref):
    for r in range(0, 128, 32):
        e = tensor_entries(rows(r, 32), [panel_ref[c : c + 1, :] for c in range(3)])
        parts = {(i, j): parts_of(e[i, j], ROW) for i in range(3) for j in range(i, 3)}
        for i in range(3):
            at = slice(128 * i + r, 128 * i + r + 32)
            for j in range(3):
                hi, whole, rest = parts[min(i, j), max(i, j)]
                hi_ref[at, 256 * j : 256 * j + 256] = hi
                f8_ref[at, 512 * j : 512 * j + 256] = whole.astype(F8)
                f8_ref[at, 512 * j + 256 : 512 * j + 512] = rest.astype(F8)


def col_store(v, dst, chi, cf8):
    for n in range(3):
        hi, whole, rest = parts_of(v[:, 256 * n : 256 * n + 256], COL)
        whole = jnp.clip(whole, -F8_MAX, F8_MAX).astype(F8)
        rest = jnp.clip(rest, -F8_MAX, F8_MAX).astype(F8)
        for j in range(3):
            rows, part = slice(dst + 256 * j, dst + 256 * j + 128), slice(128 * j, 128 * j + 128)
            chi[rows, 256 * n : 256 * n + 256] = hi[part]
            cf8[rows, 512 * n : 512 * n + 256] = rest[part]
            cf8[rows, 512 * n + 256 : 512 * n + 512] = whole[part]


def kernel(slot_ref, panel_ref, g_ref, xcat, l_in, l_out, own_out, out_ref, own_ref, wcat, chi, cf8, rhi0, rhi1, rf80, rf81, bcat, ocat, rowt, colt, colp, obuf, l_sem, own_sem, o_sem, ids):
    prow, pcol = ids()
    l_copy = pltpu.make_async_copy(l_in, l_out, l_sem)
    own_copy = pltpu.make_async_copy(own_ref, own_out, own_sem)
    l_copy.start()

    def out_copy(at_step, half):
        rows = pl.ds(128 * half, 128)
        return pltpu.make_async_copy(obuf.at[at_step % 2, half], out_ref.at[at_step, :, rows, :], o_sem.at[at_step % 2, half])

    panel_cols = lambda: [panel_ref[c : c + 1, :] for c in range(3)]

    def row_coords(tile):
        at = pl.multiple_of(tile * 128, 128)
        return lambda r, m: [rowt[pl.ds(at + r, m), k : k + 1] for k in range(3)]

    def inverse_of_diag():
        for b in range(3):
            for a in range(3):
                k = slice(256 * max(a, b), 768)
                hi = lambda q: xcat[k, 768 * q : 768 * q + 256]
                lo = lambda q: xcat[k, 768 * q + 512 : 768 * q + 768]
                w = pre_split_dot((hi(a), lo(a)), (hi(b), lo(b)), TN)
                wh, wl = split(w)
                at = slice(256 * b, 256 * b + 256)
                wcat[768 * a : 768 * a + 256, at] = wh
                wcat[768 * a + 256 : 768 * a + 512, at] = wh
                wcat[768 * a + 512 : 768 * a + 768, at] = wl

    def own_rows():
        for h in range(3):
            piece = (pcol % 4) * 3 + h
            comp, quarter = piece // 4, piece % 4
            at = pl.multiple_of((pcol // 4) * 256 + quarter * 64, 64)
            for r in range(0, 64, 32):
                diff, iso, directed = pair_terms([rowt[pl.ds(at + r, 32), k : k + 1] for k in range(3)], panel_cols())
                g = directed * jnp.where(comp == 0, diff[0], jnp.where(comp == 1, diff[1], diff[2]))
                for j in range(3):
                    hi, lo = split(g * diff[j] + jnp.where(comp == j, iso, 0.0))
                    cat_store(ocat, slice(64 * h + r, 64 * h + r + 32), j, hi, lo, "hlh")
        for n in range(3):
            k = 768 * (n + 1)
            own_ref[:, 256 * n : 256 * n + 256] = lax.dot_general(
                ocat[:, :k], xcat[256 * n : 256 * n + 256, :k], NT, preferred_element_type=F32
            )

    def rows_of(i, _):
        rowt[pl.ds(pl.multiple_of(i * 128, 128), 128), :] = transposed(lane_tile(g_ref, slot_ref[prow * 4 + i // 2], i % 2))
        return 0

    lax.fori_loop(0, 8, rows_of, 0)
    for i in range(4):
        tile = lane_tile(g_ref, slot_ref[pcol * 2 + i // 2], i % 2)
        colp[:, 128 * i : 128 * i + 128] = tile
        colt[128 * i : 128 * i + 128, :] = transposed(tile)
    inverse_of_diag()
    for i in range(4):
        buf = bcat.at[i % 2]
        panel_entries(lambda r, m: [colt[128 * i + r : 128 * i + r + m, c : c + 1] for c in range(3)], panel_ref, buf)
        v = lax.dot_general(buf[...], wcat[...], NN, preferred_element_type=F32)
        col_store(v, (i // 2) * 768 + (i % 2) * 128, chi, cf8)
    own_rows()
    own_copy.start()
    row_parts(row_coords(0), panel_ref, rhi0, rf80)

    def trailing(step, slot, which, c):
        coords = row_coords(2 * step + which)
        at = 768 * c
        v = lax.dot_general((rhi0, rhi1)[which][...], chi[at : at + 768, :], NT, preferred_element_type=F32)
        v = v + lax.dot_general((rf80, rf81)[which][...], cf8[at : at + 768, :], NT, preferred_element_type=F32)
        obuf[slot, which, :, :, at : at + 768] = v.reshape(3, 128, 768)
        for r in range(0, 128, 32):
            e = tensor_entries(coords(r, 32), [colp[k : k + 1, 256 * c : 256 * c + 256] for k in range(3)])
            for i in range(3):
                for j in range(3):
                    dst = (slot, which, i, slice(r, r + 32), slice(768 * c + 256 * j, 768 * c + 256 * j + 256))
                    obuf[dst] = e[i, j] - obuf[dst] * BACK

    def two_tiles(step, _):
        slot = step % 2

        @pl.when(step >= 2)
        def _():
            for half in range(2):
                out_copy(step - 2, half).wait()

        trailing(step, slot, 0, 0)
        row_parts(row_coords(2 * step + 1), panel_ref, rhi1, rf81)
        trailing(step, slot, 0, 1)
        out_copy(step, 0).start()
        trailing(step, slot, 1, 0)
        row_parts(row_coords(jnp.minimum(2 * step + 2, 7)), panel_ref, rhi0, rf80)
        trailing(step, slot, 1, 1)
        out_copy(step, 1).start()
        return 0

    lax.fori_loop(0, 4, two_tiles, 0)
    for step in (2, 3):
        for half in range(2):
            out_copy(step, half).wait()
    own_copy.wait()
    l_copy.wait()


def main_call(slot_block, panel_pos, gathered, xcat, factor, ids):
    whole = pl.BlockSpec(memory_space=pltpu.VMEM)
    anywhere = pl.BlockSpec(memory_space=pl.ANY)
    vmem = lambda shape, dtype: pltpu.VMEM(shape, dtype)
    l, own, out = pl.pallas_call(
        functools.partial(kernel, ids=ids),
        in_specs=[pl.BlockSpec(memory_space=pltpu.SMEM), whole, whole, whole, whole],
        out_specs=[anywhere] * 3,
        out_shape=[
            jax.ShapeDtypeStruct((768, 768), F32),
            jax.ShapeDtypeStruct((192, 768), F32),
            jax.ShapeDtypeStruct((4, 3, 256, 1536), F32),
        ],
        scratch_shapes=[
            vmem((192, 768), F32),
            vmem((2304, 768), BF16),
            vmem((1536, 768), BF16),
            vmem((1536, 1536), F8),
            vmem((384, 768), BF16),
            vmem((384, 768), BF16),
            vmem((384, 1536), F8),
            vmem((384, 1536), F8),
            vmem((2, 384, 2304), BF16),
            vmem((192, 2304), BF16),
            vmem((1024, 128), F32),
            vmem((512, 128), F32),
            vmem((8, 512), F32),
            vmem((2, 2, 3, 128, 1536), F32),
            pltpu.SemaphoreType.DMA,
            pltpu.SemaphoreType.DMA,
            pltpu.SemaphoreType.DMA((2, 2)),
        ],
        compiler_params=pltpu.CompilerParams(vmem_limit_bytes=40 << 20),
        cost_estimate=pl.CostEstimate(flops=3 * 10**10, bytes_accessed=3 * 10**7, transcendentals=0),
        name="panel_rows_and_trailing",
    )(slot_block, panel_pos, gathered, xcat, factor)
    return l, own, out.reshape(3072, 1536)


def shards(panel_pos, trail_pos, slot_block):
    factor, xcat, gathered, panel8 = front_call(panel_pos, trail_pos)
    return main_call(slot_block, panel8, gathered, xcat, factor, lambda: (lax.axis_index("prow"), lax.axis_index("pcol")))


def solution(mesh):
    return jax.shard_map(
        shards,
        mesh=mesh,
        in_specs=(P(), P(None, ("prow", "pcol")), P()),
        out_specs=(P(), P(("prow", "pcol"), None), P("prow", "pcol")),
        check_vma=False,
    )
```

```python
import functools
import jax
import jax.numpy as jnp
from jax import lax
from jax.experimental import pallas as pl
from jax.experimental.pallas import tpu as pltpu
from jax.sharding import PartitionSpec as P

RADIUS = 0.25
F32, BF16, F8 = jnp.float32, jnp.bfloat16, jnp.float8_e4m3fn
NT = (((1,), (1,)), ((), ()))
NN = (((1,), (0,)), ((), ()))
TN = (((0,), (0,)), ((), ()))


def split(x):
    hi = x.astype(BF16)
    return hi, (x - hi.astype(F32)).astype(BF16)


def dot3(a, b, dims):
    ah, al = split(a)
    bh, bl = split(b)
    d = functools.partial(lax.dot_general, dimension_numbers=dims, preferred_element_type=F32)
    return d(ah, bh) + (d(al, bh) + d(ah, bl))


def pair_terms(rows, cols):
    diff = [r - c for r, c in zip(rows, cols)]
    squared = diff[0] * diff[0] + diff[1] * diff[1] + diff[2] * diff[2]
    same = squared < 0.01
    inv = lax.rsqrt(jnp.where(same, 1.0, squared))
    inv2 = inv * inv
    t = (0.75 * RADIUS) * inv
    t2 = t * inv2
    iso = jnp.where(same, 1.0, t + (RADIUS * RADIUS * 2.0 / 3.0) * t2)
    directed = t2 * (1.0 - (2.0 * RADIUS * RADIUS) * inv2)
    return diff, iso, directed


def tensor_entries(rows, cols):
    diff, iso, directed = pair_terms(rows, cols)
    g = [directed * d for d in diff]
    e = {}
    for i in range(3):
        for j in range(i, 3):
            v = g[i] * diff[j]
            if i == j:
                v = v + iso
            e[i, j] = e[j, i] = v
    return e


def bsub(row):
    return jnp.broadcast_to(row, (8, row.shape[-1]))


def rep(tile, rows):
    return jnp.concatenate([tile] * (rows // 8), axis=0)


def first_tile(tile, rest):
    return tile if rest.shape[0] == 8 else jnp.concatenate([tile, rest[8:]], axis=0)


def factor_block(d_ref):
    sub = lax.broadcasted_iota(jnp.int32, (8, 128), 0)
    a = d_ref[:, :128]
    inv = d_ref[:, 128:]
    for t in range(16):
        n = 128 - 8 * t
        cs = [jnp.broadcast_to(a[:, 8 * t + k : 8 * t + k + 1], (n, 128)) for k in range(8)]
        for j in range(8):
            rs = lax.rsqrt(bsub(cs[j][j : j + 1, :]))
            m = cs[j] * rep(rs, n)
            sp = [rep(bsub(m[k : k + 1, :]), n) for k in range(j + 1, 8)]
            m = first_tile(jnp.where(sub > j, m[:8], 0.0), m)
            ua = bsub(a[j : j + 1, :]) * rs
            ui = bsub(inv[j : j + 1, :]) * rs
            a = a - m * rep(ua, n)
            a = first_tile(jnp.where(sub == j, ua, a[:8]), a)
            inv = inv - m * rep(ui, n)
            inv = first_tile(jnp.where(sub == j, ui, inv[:8]), inv)
            for k in range(j + 1, 8):
                cs[k] = cs[k] - m * sp[k - j - 1]
        d_ref[8 * t : 8 * t + 8, :128] = a[:8]
        d_ref[8 * t : 8 * t + 8, 128:] = inv[:8]
        if t < 15:
            a, inv = a[8:], inv[8:]


def cat_store(ref, rows, chunk, hi, lo, order):
    base = 768 * chunk
    for i, w in enumerate(order):
        ref[rows, base + 256 * i : base + 256 * i + 256] = hi if w == "h" else lo


def pre_split_dot(a, b, dims):
    d = functools.partial(lax.dot_general, dimension_numbers=dims, preferred_element_type=F32)
    return d(a[0], b[0]) + (d(a[1], b[0]) + d(a[0], b[1]))


def chol(panel_ref, panel_t, m_ref, d_ref, row_buf, lt_buf, l_buf, xcat, after):
    m_ref[128:768, 768:1408] = jnp.zeros((640, 640), F32)
    for r in range(0, 256, 32):
        rows = [panel_t[r : r + 32, c : c + 1] for c in range(3)]
        cols = [panel_ref[c : c + 1, :] for c in range(3)]
        e = tensor_entries(rows, cols)
        for i in range(3):
            for j in range(3):
                m_ref[256 * i + r : 256 * i + r + 32, 256 * j : 256 * j + 256] = e[i, j]
    rows_at = lax.broadcasted_iota(jnp.int32, (128, 128), 0)
    cols_at = lax.broadcasted_iota(jnp.int32, (128, 128), 1)
    eye = (rows_at == cols_at).astype(F32)
    row_buf[...] = jnp.zeros(row_buf.shape, F32)
    lt_buf[...] = jnp.zeros(lt_buf.shape, F32)
    d_ref[:, :128] = m_ref[:128, :128]
    d_ref[:, 128:] = eye

    def panel(p, _):
        base = pl.multiple_of(128 * p, 128)
        nxt = pl.multiple_of(128 * p + 128, 128)
        row_parts = split(row_buf[...])
        for i in range(5):
            at = pl.multiple_of(base + 128 * i, 128)
            lt_parts = split(lt_buf[128 * i : 128 * i + 128, :])
            m_ref[pl.ds(at, 128), pl.ds(base, 768)] -= pre_split_dot(lt_parts, row_parts, NN)
        factor_block(d_ref)
        x = d_ref[:, 128:]
        l_buf[pl.ds(base, 128), pl.ds(base, 128)] = jnp.where(rows_at >= cols_at, d_ref[:, :128].T, 0.0)
        row = dot3(x, m_ref[pl.ds(base, 128), pl.ds(nxt, 640)], NN)
        row_buf[:, :640] = row
        row_buf[:, 640:] = x
        m_ref[pl.ds(base, 128), pl.ds(nxt, 640)] = row
        m_ref[pl.ds(base, 128), pl.ds(768 + base, 128)] = x
        first = row[:, :128].T
        d_ref[:, :128] = m_ref[pl.ds(nxt, 128), pl.ds(nxt, 128)] - dot3(first, row[:, :128], NN)
        d_ref[:, 128:] = eye
        lt_buf[:128, :] = first
        l_buf[pl.ds(nxt, 128), pl.ds(base, 128)] = first
        for i in range(1, 5):
            lt = row[:, 128 * i : 128 * i + 128].T
            lt_buf[128 * i : 128 * i + 128, :] = lt
            l_buf[pl.ds(pl.multiple_of(nxt + 128 * i, 128), 128), pl.ds(base, 128)] = lt
        after(p)
        return 0

    lax.fori_loop(0, 6, panel, 0)
    for q in range(6):
        rows = slice(128 * q, 128 * q + 128)
        for c in range(6):
            zero = jnp.zeros((128, 128), BF16)
            hi, lo = (zero, zero) if c > q else split(m_ref[rows, 768 + 128 * c : 896 + 128 * c])
            at = 768 * (c // 2) + 128 * (c % 2)
            xcat[rows, at : at + 128] = hi
            xcat[rows, at + 256 : at + 384] = hi
            xcat[rows, at + 512 : at + 640] = lo


def store_factor(l_ref, l_buf):
    for q in range(6):
        rows = slice(128 * q, 128 * q + 128)
        l_ref[rows, : 128 * q + 128] = l_buf[rows, : 128 * q + 128]
        if q < 5:
            l_ref[rows, 128 * q + 128 :] = jnp.zeros((128, 640 - 128 * q), F32)


def lane_tile(g_ref, k, half):
    tiles = []
    for d in (4 * k + 2 * half, 4 * k + 2 * half + 1):
        tiles.append(jnp.concatenate([g_ref[d % 16, d // 16][:, :64], jnp.zeros((5, 64), F32)], axis=0))
    return jnp.concatenate(tiles, axis=1)


def transposed(tile):
    return jnp.concatenate([tile, jnp.zeros((120, 128), F32)], axis=0).T


MESH = pl.DeviceIdType.MESH


def front_kernel(x_ref, l_ref, xcat, g_ref, p8, m_ref, d_ref, row_buf, lt_buf, l_buf, pt, send_sem, recv_sem, local_sem):
    r = lax.axis_index("prow")
    c = lax.axis_index("pcol")
    core, z, y, x = r % 2, r // 2, c % 4, c // 4
    own_ref = x_ref.at[:, 256:384]
    local = pltpu.make_async_copy(own_ref, g_ref.at[c, r], local_sem)
    local.start()
    pair, line, plane = g_ref.at[c, pl.ds(2 * z, 2)], g_ref.at[c], g_ref.at[pl.ds(4 * x, 4)]
    plan = [
        [(own_ref, g_ref.at[c, r], (r + 1 - 2 * core, c))],
        [(pair, pair, (lax.rem(z + i, 4) * 2 + core, c)) for i in range(1, 4)],
        [(line, line, (r, x * 4 + lax.rem(y + i, 4))) for i in range(1, 4)],
        [(plane, plane, (r, lax.rem(x + i, 4) * 4 + y)) for i in range(1, 4)],
    ]
    barrier = pltpu.get_barrier_semaphore()
    for stage in plan:
        for _, _, target in stage:
            pl.semaphore_signal(barrier, inc=1, device_id=target, device_id_type=MESH)

    stages = []
    for k, stage in enumerate(plan):
        stages.append([
            pltpu.make_async_remote_copy(
                src_ref=src,
                dst_ref=dst,
                send_sem=send_sem.at[3 * k + i],
                recv_sem=recv_sem.at[3 * k + i],
                device_id=target,
                device_id_type=MESH,
            )
            for i, (src, dst, target) in enumerate(stage)
        ])

    def after(p):
        @pl.when(p == 0)
        def _():
            pl.semaphore_wait(barrier, 10)
            for copy in stages[0]:
                copy.start()

        for k in range(1, 4):

            @pl.when(p == k)
            def _():
                if k == 1:
                    local.wait()
                for copy in stages[k - 1]:
                    copy.wait()
                for copy in stages[k]:
                    copy.start()

    p8[...] = jnp.zeros((8, 256), F32)
    p8[:3, :] = x_ref[:, :256]
    for half in range(2):
        pt[128 * half : 128 * half + 128, :] = transposed(p8[:, 128 * half : 128 * half + 128])
    chol(p8, pt, m_ref, d_ref, row_buf, lt_buf, l_buf, xcat, after)
    store_factor(l_ref, l_buf)
    for copy in stages[3]:
        copy.wait()


def front_call(panel_pos, own):
    vmem = pl.BlockSpec(memory_space=pltpu.VMEM)
    together = jnp.concatenate([panel_pos, jnp.pad(own, ((0, 0), (0, 128 - own.shape[1])))], axis=1)
    return pl.pallas_call(
        front_kernel,
        out_shape=[
            jax.ShapeDtypeStruct((768, 768), F32),
            jax.ShapeDtypeStruct((768, 2304), BF16),
            jax.ShapeDtypeStruct((16, 8, 3, 128), F32),
            jax.ShapeDtypeStruct((8, 256), F32),
        ],
        in_specs=[vmem],
        out_specs=[vmem] * 4,
        cost_estimate=pl.CostEstimate(flops=10**10, bytes_accessed=10**7, transcendentals=0),
        scratch_shapes=[
            pltpu.VMEM((1280, 1536), F32),
            pltpu.VMEM((128, 256), F32),
            pltpu.VMEM((128, 768), F32),
            pltpu.VMEM((640, 128), F32),
            pltpu.VMEM((1408, 768), F32),
            pltpu.VMEM((256, 128), F32),
            pltpu.SemaphoreType.DMA((12,)),
            pltpu.SemaphoreType.DMA((12,)),
            pltpu.SemaphoreType.DMA,
        ],
        compiler_params=pltpu.CompilerParams(collective_id=0, has_side_effects=True, vmem_limit_bytes=40 << 20),
        name="factor_and_gather",
    )(together)


def panel_entries(rows, panel_ref, bcat):
    for r in range(0, 128, 32):
        e = tensor_entries(rows(r, 32), [panel_ref[c : c + 1, :] for c in range(3)])
        for i in range(3):
            for j in range(3):
                hi, lo = split(e[i, j])
                cat_store(bcat, slice(128 * i + r, 128 * i + r + 32), j, hi, lo, "hlh")


ROW = (2048.0, 256.0, 131072.0)
COL = (1024.0, 16.0, 8192.0)
BACK = 1.0 / (2048.0 * 1024.0)
F8_MAX = 448.0


def parts_of(v, scales):
    scaled = v * scales[0]
    hi = scaled.astype(BF16)
    rest = scaled - hi.astype(F32)
    return hi, scaled * (scales[1] / scales[0]), rest * (scales[2] / scales[0])


def row_parts(rows, panel_ref, hi_ref, f8_ref):
    for r in range(0, 128, 32):
        e = tensor_entries(rows(r, 32), [panel_ref[c : c + 1, :] for c in range(3)])
        parts = {(i, j): parts_of(e[i, j], ROW) for i in range(3) for j in range(i, 3)}
        for i in range(3):
            at = slice(128 * i + r, 128 * i + r + 32)
            for j in range(3):
                hi, whole, rest = parts[min(i, j), max(i, j)]
                hi_ref[at, 256 * j : 256 * j + 256] = hi
                f8_ref[at, 512 * j : 512 * j + 256] = whole.astype(F8)
                f8_ref[at, 512 * j + 256 : 512 * j + 512] = rest.astype(F8)


def col_store(v, dst, chi, cf8):
    for n in range(3):
        hi, whole, rest = parts_of(v[:, 256 * n : 256 * n + 256], COL)
        whole = jnp.clip(whole, -F8_MAX, F8_MAX).astype(F8)
        rest = jnp.clip(rest, -F8_MAX, F8_MAX).astype(F8)
        for j in range(3):
            rows, part = slice(dst + 256 * j, dst + 256 * j + 128), slice(128 * j, 128 * j + 128)
            chi[rows, 256 * n : 256 * n + 256] = hi[part]
            cf8[rows, 512 * n : 512 * n + 256] = rest[part]
            cf8[rows, 512 * n + 256 : 512 * n + 512] = whole[part]


def kernel(slot_ref, panel_ref, g_ref, xcat, l_in, l_out, own_out, out_ref, own_ref, wcat, chi, cf8, rhi0, rhi1, rf80, rf81, bcat, ocat, rowt, colt, colp, obuf, l_sem, own_sem, o_sem, ids):
    prow, pcol = ids()
    l_copy = pltpu.make_async_copy(l_in, l_out, l_sem)
    own_copy = pltpu.make_async_copy(own_ref, own_out, own_sem)
    l_copy.start()

    def out_copy(at_step, half):
        rows = pl.ds(128 * half, 128)
        return pltpu.make_async_copy(obuf.at[at_step % 2, half], out_ref.at[at_step, :, rows, :], o_sem.at[at_step % 2, half])

    panel_cols = lambda: [panel_ref[c : c + 1, :] for c in range(3)]

    def row_coords(tile):
        at = pl.multiple_of(tile * 128, 128)
        return lambda r, m: [rowt[pl.ds(at + r, m), k : k + 1] for k in range(3)]

    def inverse_of_diag():
        for b in range(3):
            for a in range(b + 1):
                k = slice(256 * b, 768)
                hi = lambda q: xcat[k, 768 * q : 768 * q + 256]
                lo = lambda q: xcat[k, 768 * q + 512 : 768 * q + 768]
                w = pre_split_dot((hi(a), lo(a)), (hi(b), lo(b)), TN)
                for row, col, block in [(a, b, w)] + ([(b, a, w.T)] if a < b else []):
                    wh, wl = split(block)
                    at = slice(256 * col, 256 * col + 256)
                    wcat[768 * row : 768 * row + 256, at] = wh
                    wcat[768 * row + 256 : 768 * row + 512, at] = wh
                    wcat[768 * row + 512 : 768 * row + 768, at] = wl

    def own_rows():
        for h in range(3):
            piece = (pcol % 4) * 3 + h
            comp, quarter = piece // 4, piece % 4
            at = pl.multiple_of((pcol // 4) * 256 + quarter * 64, 64)
            for r in range(0, 64, 32):
                diff, iso, directed = pair_terms([rowt[pl.ds(at + r, 32), k : k + 1] for k in range(3)], panel_cols())
                g = directed * jnp.where(comp == 0, diff[0], jnp.where(comp == 1, diff[1], diff[2]))
                for j in range(3):
                    hi, lo = split(g * diff[j] + jnp.where(comp == j, iso, 0.0))
                    cat_store(ocat, slice(64 * h + r, 64 * h + r + 32), j, hi, lo, "hlh")
        for n in range(3):
            k = 768 * (n + 1)
            own_ref[:, 256 * n : 256 * n + 256] = lax.dot_general(
                ocat[:, :k], xcat[256 * n : 256 * n + 256, :k], NT, preferred_element_type=F32
            )

    def rows_of(i, _):
        rowt[pl.ds(pl.multiple_of(i * 128, 128), 128), :] = transposed(lane_tile(g_ref, slot_ref[prow * 4 + i // 2], i % 2))
        return 0

    lax.fori_loop(0, 8, rows_of, 0)
    for i in range(4):
        tile = lane_tile(g_ref, slot_ref[pcol * 2 + i // 2], i % 2)
        colp[:, 128 * i : 128 * i + 128] = tile
        colt[128 * i : 128 * i + 128, :] = transposed(tile)
    inverse_of_diag()
    for i in range(4):
        buf = bcat.at[i % 2]
        panel_entries(lambda r, m: [colt[128 * i + r : 128 * i + r + m, c : c + 1] for c in range(3)], panel_ref, buf)
        v = lax.dot_general(buf[...], wcat[...], NN, preferred_element_type=F32)
        col_store(v, (i // 2) * 768 + (i % 2) * 128, chi, cf8)
    own_rows()
    own_copy.start()
    row_parts(row_coords(0), panel_ref, rhi0, rf80)

    def trailing(step, slot, which, c):
        coords = row_coords(2 * step + which)
        at = 768 * c
        v = lax.dot_general((rhi0, rhi1)[which][...], chi[at : at + 768, :], NT, preferred_element_type=F32)
        v = v + lax.dot_general((rf80, rf81)[which][...], cf8[at : at + 768, :], NT, preferred_element_type=F32)
        obuf[slot, which, :, :, at : at + 768] = v.reshape(3, 128, 768)
        for r in range(0, 128, 32):
            e = tensor_entries(coords(r, 32), [colp[k : k + 1, 256 * c : 256 * c + 256] for k in range(3)])
            for i in range(3):
                for j in range(3):
                    dst = (slot, which, i, slice(r, r + 32), slice(768 * c + 256 * j, 768 * c + 256 * j + 256))
                    obuf[dst] = e[i, j] - obuf[dst] * BACK

    def two_tiles(step, _):
        slot = step % 2

        @pl.when(step >= 2)
        def _():
            for half in range(2):
                out_copy(step - 2, half).wait()

        trailing(step, slot, 0, 0)
        row_parts(row_coords(2 * step + 1), panel_ref, rhi1, rf81)
        trailing(step, slot, 0, 1)
        out_copy(step, 0).start()
        trailing(step, slot, 1, 0)
        row_parts(row_coords(jnp.minimum(2 * step + 2, 7)), panel_ref, rhi0, rf80)
        trailing(step, slot, 1, 1)
        out_copy(step, 1).start()
        return 0

    lax.fori_loop(0, 4, two_tiles, 0)
    for step in (2, 3):
        for half in range(2):
            out_copy(step, half).wait()
    own_copy.wait()
    l_copy.wait()


def main_call(slot_block, panel_pos, gathered, xcat, factor, ids):
    whole = pl.BlockSpec(memory_space=pltpu.VMEM)
    anywhere = pl.BlockSpec(memory_space=pl.ANY)
    vmem = lambda shape, dtype: pltpu.VMEM(shape, dtype)
    l, own, out = pl.pallas_call(
        functools.partial(kernel, ids=ids),
        in_specs=[pl.BlockSpec(memory_space=pltpu.SMEM), whole, whole, whole, whole],
        out_specs=[anywhere] * 3,
        out_shape=[
            jax.ShapeDtypeStruct((768, 768), F32),
            jax.ShapeDtypeStruct((192, 768), F32),
            jax.ShapeDtypeStruct((4, 3, 256, 1536), F32),
        ],
        scratch_shapes=[
            vmem((192, 768), F32),
            vmem((2304, 768), BF16),
            vmem((1536, 768), BF16),
            vmem((1536, 1536), F8),
            vmem((384, 768), BF16),
            vmem((384, 768), BF16),
            vmem((384, 1536), F8),
            vmem((384, 1536), F8),
            vmem((2, 384, 2304), BF16),
            vmem((192, 2304), BF16),
            vmem((1024, 128), F32),
            vmem((512, 128), F32),
            vmem((8, 512), F32),
            vmem((2, 2, 3, 128, 1536), F32),
            pltpu.SemaphoreType.DMA,
            pltpu.SemaphoreType.DMA,
            pltpu.SemaphoreType.DMA((2, 2)),
        ],
        compiler_params=pltpu.CompilerParams(vmem_limit_bytes=40 << 20),
        cost_estimate=pl.CostEstimate(flops=3 * 10**10, bytes_accessed=3 * 10**7, transcendentals=0),
        name="panel_rows_and_trailing",
    )(slot_block, panel_pos, gathered, xcat, factor)
    return l, own, out.reshape(3072, 1536)


def shards(panel_pos, trail_pos, slot_block):
    factor, xcat, gathered, panel8 = front_call(panel_pos, trail_pos)
    return main_call(slot_block, panel8, gathered, xcat, factor, lambda: (lax.axis_index("prow"), lax.axis_index("pcol")))


def solution(mesh):
    return jax.shard_map(
        shards,
        mesh=mesh,
        in_specs=(P(), P(None, ("prow", "pcol")), P()),
        out_specs=(P(), P(("prow", "pcol"), None), P("prow", "pcol")),
        check_vma=False,
    )
```
